256 devices in a mesh: tile: 128 (over y, z, x), sub: 2 (over core).
Axes of the slice: x: 4, y: 4, z: 8, core: 2. Of those that a mesh axis runs over, the one named last changes fastest.
Arguments:
- right_side: float32 [2, 32768, 256], P(None, ('tile', 'sub')), may hold values from -12 to 12
- pixel_weight: float32 [32768, 256], P(('tile', 'sub')), may hold values from 0.5 to 2
- noise_diag: float32 [2, 32768, 256], P(None, ('tile', 'sub')), may hold values from 0.5 to 8
- noise_corr: float32 [32768, 256], P(('tile', 'sub')), may hold values from -0.8 to 0.8
- neighbours: int32 [3, 4, 128], replicated, may hold values from 0 to 127, as said below
Outputs:
- solution: float32 [2, 32768, 256], P(None, ('tile', 'sub'))
- final_misfit: float32 [2, 32768, 256], P(None, ('tile', 'sub'))
The draws below stay inside these ranges and needn't reach their ends.
Inputs may be any that keep to these rules, and one draw needn't show every extreme that they name: `neighbours`: across side 0 lies side 1 of another or the same tile and across side 2 lies side 3, and conversely; the relation is symmetric, with the same reversal flag on both sides of an edge. Every neighbour lies, in the cyclic order of tiles, within 3 places of its tile or within 3 places of the tile 128/2 places away, and 3 places is reached. Flags are 0 or 1.
All inputs are finite; a program needn't handle non-finite values.
Results may differ from the reference program's by a relative error of at most 0.00012.
Values sent between devices are 32-bit elements; how exact they have to be, the bound alone decides.
A program may use at most 128 MiB of HBM per device.

```python
import math
import jax
import jax.numpy as jnp

TS = 256
NU = 2
NC = 3
TILES = 128
ROWS = 32768


def neighbour_tables(key):
    base_key = jax.random.fold_in(key, 7)
    first_key, second_key, third_key, fourth_key = jax.random.split(base_key, 4)
    blocks = TILES // 4
    half_cycle = TILES // 2
    block_ids = jnp.arange(blocks, dtype=jnp.int32)

    def block_order(sub_key, block_index):
        return jax.random.permutation(jax.random.fold_in(sub_key, block_index), 4).astype(jnp.int32)
    vertical = jax.vmap(lambda block_index: block_order(first_key, block_index))(block_ids)
    vertical = vertical.at[0].set(jnp.array([3, 2, 1, 0], jnp.int32))
    lateral = jax.vmap(lambda block_index: block_order(second_key, block_index))(block_ids)
    positions = jnp.arange(TILES, dtype=jnp.int32)
    below_tile = (block_ids[:, None] * 4 + vertical).reshape(-1).astype(jnp.int32)
    starts = ((block_ids[:, None] * 4 + jnp.arange(4, dtype=jnp.int32)[None, :] + 2) % TILES).reshape(-1)
    targets = ((block_ids[:, None] * 4 + lateral + 2 + half_cycle) % TILES).reshape(-1)
    beside = jnp.zeros(TILES, jnp.int32).at[starts].set(targets.astype(jnp.int32))
    above_tile = jnp.zeros(TILES, jnp.int32).at[below_tile].set(positions)
    leftward = jnp.zeros(TILES, jnp.int32).at[beside].set(positions)
    flip_vertical = jax.random.randint(third_key, (TILES,), 0, 2).astype(jnp.int32)
    flip_lateral = jax.random.randint(fourth_key, (TILES,), 0, 2).astype(jnp.int32)
    tile_ids = jnp.stack([above_tile, below_tile, leftward, beside])
    ones_row = jnp.ones(TILES, jnp.int32)
    face_ids = jnp.stack([ones_row, 0 * ones_row, 3 * ones_row, 2 * ones_row])
    flip_ids = jnp.stack([flip_vertical[above_tile], flip_vertical, flip_lateral[leftward], flip_lateral])
    return jnp.stack([tile_ids, face_ids, flip_ids]).astype(jnp.int32)


def draw_neighbours(key, part):
    return neighbour_tables(key)


def steps_of(stream_key, extent, cuts, low, top_value):
    def one(axis_at, parts):
        heights = jax.random.uniform(jax.random.fold_in(jax.random.fold_in(stream_key, 6), axis_at), (parts,), jnp.float32, low / len(cuts), top_value / len(cuts))
        return jnp.repeat(jnp.exp(heights), extent[axis_at] // parts).reshape((-1,) + (1,) * (len(extent) - axis_at - 1))

    level = one(*cuts[0])
    for cut in cuts[1:]:
        level = level * one(*cut)
    return level


def gaussian(key, dims, spread, limit, shards=(), kind=jnp.bfloat16):
    entries = spread * jax.random.normal(key, dims, jnp.float32)
    if shards:
        entries = entries * steps_of(key, dims, shards, -0.22, 0.18)
    return jnp.clip(entries, -limit, limit).astype(kind)


def setup_inputs(seed: int = 0) -> dict:
    streams_of = jax.random.split(jax.random.key(seed), 6)
    return {
        "right_side": gaussian(streams_of[0], (2, ROWS, TS), 2.0, 12.0, ((1, 256),), jnp.float32),
        "pixel_weight": jnp.clip(jnp.exp(math.log(2.0) - 1.3862944 * jax.random.uniform(streams_of[1], (ROWS, TS), jnp.float32) ** steps_of(streams_of[1], (ROWS, TS), ((0, 256),), -0.2, 0.2)), 0.5, 2.0),
        "noise_diag": jnp.clip(jnp.exp(math.log(8.0) - 2.7725887 * jax.random.uniform(streams_of[2], (2, ROWS, TS), jnp.float32) ** steps_of(streams_of[2], (2, ROWS, TS), ((1, 256),), -0.2, 0.2)), 0.5, 8.0),
        "noise_corr": jnp.clip(jax.random.uniform(streams_of[3], (ROWS, TS), jnp.float32, -0.8, 0.8) * steps_of(streams_of[3], (ROWS, TS), ((0, 256),), -0.4, 0.0), -0.8, 0.8),
        "neighbours": draw_neighbours(jax.random.fold_in(streams_of[5], 71), 0),
    }


MASS = 0.05
OMEGA = 0.8

def inverse_blocks(diag_term, noise_terms):
    upper_left = diag_term + noise_terms[0]
    lower_right = diag_term + noise_terms[1]
    determinant = upper_left * lower_right - noise_terms[2] * noise_terms[2]
    return jnp.stack([lower_right / determinant, upper_left / determinant, -noise_terms[2] / determinant])

def apply_block(inverse, misfit):
    out_first = inverse[0] * misfit[0] + inverse[2] * misfit[1]
    second = inverse[2] * misfit[0] + inverse[1] * misfit[1]
    return jnp.stack([out_first, second])

def coarsen_sum(values):
    old_shape = values.shape
    new_shape = old_shape[:-2] + (old_shape[-2] // 2, 2, old_shape[-1] // 2, 2)
    return values.reshape(new_shape).sum(axis=(-3, -1))

def prolong(values):
    return jnp.repeat(jnp.repeat(values, 2, axis=-2), 2, axis=-1)

def neighbour_sum(scaled, neighbours):
    edge_rows = jnp.stack([scaled[:, :, 0, :], scaled[:, :, -1, :], scaled[:, :, :, 0], scaled[:, :, :, -1]])
    by_tile = jnp.transpose(edge_rows, (2, 0, 1, 3))
    across = by_tile[neighbours[0].T, neighbours[1].T]
    across = jnp.where(neighbours[2].T[:, :, None, None] == 1, jnp.flip(across, axis=3), across)
    across = jnp.transpose(across, (1, 2, 0, 3))
    above_rows = jnp.concatenate([across[0][:, :, None, :], scaled[:, :, :-1, :]], axis=2)
    below_rows = jnp.concatenate([scaled[:, :, 1:, :], across[1][:, :, None, :]], axis=2)
    west_cols = jnp.concatenate([across[2][:, :, :, None], scaled[:, :, :, :-1]], axis=3)
    east_cols = jnp.concatenate([scaled[:, :, :, 1:], across[3][:, :, :, None]], axis=3)
    return above_rows + below_rows + west_cols + east_cols

def operate(iterate, weight, stiffness, noise_terms, neighbours):
    scaled = weight * iterate
    stencil = (MASS + 4.0) * scaled - neighbour_sum(scaled, neighbours)
    out_first = stiffness * weight * stencil[0] + noise_terms[0] * iterate[0] + noise_terms[2] * iterate[1]
    second = stiffness * weight * stencil[1] + noise_terms[2] * iterate[0] + noise_terms[1] * iterate[1]
    return jnp.stack([out_first, second])

def relax(iterate, source, weight, stiffness, noise_terms, inverse, neighbours):
    misfit = source - operate(iterate, weight, stiffness, noise_terms, neighbours)
    return iterate + OMEGA * apply_block(inverse, misfit)

def reference(right_side, pixel_weight, noise_diag, noise_corr, neighbours):
    source = right_side.reshape(2, TILES, TS, TS)
    weight = pixel_weight.reshape(TILES, TS, TS)
    diag_pair = noise_diag.reshape(2, TILES, TS, TS)
    correlation = noise_corr.reshape(TILES, TS, TS)
    cross_noise = correlation * jnp.sqrt(diag_pair[0] * diag_pair[1])
    noise_terms = jnp.stack([diag_pair[0], diag_pair[1], cross_noise])
    inverse = inverse_blocks((MASS + 4.0) * weight * weight, noise_terms)
    iterate = OMEGA * apply_block(inverse, source)
    for sweep_no in range(NU - 1):
        iterate = relax(iterate, source, weight, 1.0, noise_terms, inverse, neighbours)
    misfit = source - operate(iterate, weight, 1.0, noise_terms, neighbours)
    coarse_source = coarsen_sum(misfit)
    coarse_weight = 0.25 * coarsen_sum(weight)
    coarse_noise = coarsen_sum(noise_terms)
    coarse_inverse = inverse_blocks(2.0 * (MASS + 4.0) * coarse_weight * coarse_weight, coarse_noise)
    correction = OMEGA * apply_block(coarse_inverse, coarse_source)
    for sweep_no in range(NC - 1):
        correction = relax(correction, coarse_source, coarse_weight, 2.0, coarse_noise, coarse_inverse, neighbours)
    iterate = iterate + prolong(correction)
    for sweep_no in range(NU):
        iterate = relax(iterate, source, weight, 1.0, noise_terms, inverse, neighbours)
    final_misfit = source - operate(iterate, weight, 1.0, noise_terms, neighbours)
    return (iterate.reshape(2, TILES * TS, TS), final_misfit.reshape(2, TILES * TS, TS))
```

```python
import functools

import jax
import jax.numpy as jnp
from jax import lax
from jax.experimental import pallas as pl
from jax.experimental.pallas import tpu as pltpu
from jax.sharding import PartitionSpec as P

MASS = 0.05
OMEGA = 0.8
KEEP = 1.0 - OMEGA
CENTRE = MASS + 4.0
TS = 256
HALF = 128
TILES = 128
CHUNK = 8
CHUNKS = TS // CHUNK
MESH = pl.DeviceIdType.MESH

LINE_OFFS = [-3, -2, -1, 1, 2, 3] + [64 + d for d in range(-3, 4)]
CORNER_OFFS = [-6, -5, -4, -3, -2, -1, 1, 2, 3, 4, 5, 6] + [64 + d for d in range(-6, 7)]


def slot_of(distance, reach):
    d = lax.rem(distance + TILES, TILES)
    far = d - (64 - reach) + 2 * reach
    near = jnp.where(d <= reach, d + reach - 1, d - (TILES - reach))
    slot = jnp.where((d <= reach) | (d >= TILES - reach), near, far)
    slot = jnp.where(d == 0, 4 * reach + 1, slot)
    return jnp.minimum(jnp.maximum(slot, 0), 4 * reach + 1)


def lanes(rows, cols):
    return lax.broadcasted_iota(jnp.int32, (rows, cols), 1)


def pair_sum(x):
    lane = lanes(CHUNK, TS)
    x = x + jnp.where(lane % 2 == 0, pltpu.roll(x, TS - 1, 1), pltpu.roll(x, 1, 1))
    row = lax.broadcasted_iota(jnp.int32, (CHUNK, TS), 0)
    return x + jnp.where(row % 2 == 0, pltpu.roll(x, CHUNK - 1, 0), pltpu.roll(x, 1, 0))


def smoother_terms(stiffness, w, n0, n1, cross, f0, f1):
    diag = (stiffness * CENTRE) * w * w
    b00, b11 = diag + n0, diag + n1
    scale = OMEGA / (b00 * b11 - cross * cross)
    k00, k11, k01 = scale * b11, scale * b00, -(scale * cross)
    v0 = w * (k00 * f0 + k01 * f1)
    v1 = w * (k01 * f0 + k11 * f1)
    ww = stiffness * w * w
    return v0, v1, ww * k00, ww * k11, ww * k01


def kernel(
    nb, rs_in, w_in, nd_in, nc_in, sol_out, mis_out,
    rs, wt, nd, nc, iw, kf, kc, sf, sc, wiw, va, vb, ca, cb,
    ec, ect, hs, hc, st1, st2, st3, st4, re1, re2, re3, re4, nb1, nb2, nb3, nb4,
    cs1, cs2, cs3, cr1, cr2, cr3, lsem, psem, prem, ssem, rsem, cssem, crsem,
):
    cst, cre = (cs1, cs2, cs3), (cr1, cr2, cr3)
    t = lax.axis_index("tile")
    c = lax.axis_index("sub")
    band = pl.multiple_of(c * HALF, HALF)

    def tile_at(offset):
        return (lax.rem(t + (offset + TILES), TILES), c)

    barrier = pltpu.get_barrier_semaphore()
    for o in CORNER_OFFS:
        pl.semaphore_signal(barrier, inc=1, device_id=tile_at(o), device_id_type=MESH)
    pl.semaphore_signal(barrier, inc=1, device_id=(t, 1 - c), device_id_type=MESH)

    rows = pl.ds(band, HALF)
    moves = [
        (rs_in.at[0], rs.at[0, rows]), (rs_in.at[1], rs.at[1, rows]), (w_in, wt.at[rows]),
        (nd_in.at[0], nd.at[0, rows]), (nd_in.at[1], nd.at[1, rows]), (nc_in, nc.at[rows]),
    ]
    local = [pltpu.make_async_copy(s, d, lsem.at[i]) for i, (s, d) in enumerate(moves)]
    for m in local:
        m.start()
    pl.semaphore_wait(barrier, len(CORNER_OFFS) + 1)
    shared = [
        pltpu.make_async_remote_copy(
            s, d, psem.at[i], prem.at[i], device_id=(t, 1 - c), device_id_type=MESH
        )
        for i, (s, d) in enumerate(moves)
    ]
    for m in shared:
        m.start()

    flip, line_slot, ghost = [], [], {}
    for k in range(4):
        n, f = nb[0, k, t], nb[2, k, t]
        flip.append(f)
        line_slot.append(slot_of(n - t, 3))
        base = 2 if k < 2 else 0
        for e in range(2):
            end = jnp.where(f == 1, 1 - e, e)
            q = base + end
            m, g = nb[0, q, n], nb[2, q, n]
            place = (k ^ 1) % 2
            ghost[k, e] = (slot_of(m - t, 6), end, jnp.where(g == 1, 1 - place, place))

    def send(x, stage, land, width):
        for o in LINE_OFFS:
            i = LINE_OFFS.index((-o + 3) % TILES - 3)
            pltpu.make_async_remote_copy(
                stage, land.at[i], ssem.at[x], rsem.at[x], device_id=tile_at(o), device_id_type=MESH
            ).start()
        if x < 3:
            lane = lanes(2, HALF)
            for k in range(4):
                pair = stage[k, 0:2, :]
                cst[x][2 * k : 2 * k + 2, :] = jnp.where(lane < 64, pair[:, :HALF], pair[:, HALF:])
            for o in CORNER_OFFS:
                i = CORNER_OFFS.index((-o + 6) % TILES - 6)
                pltpu.make_async_remote_copy(
                    cst[x], cre[x].at[i], cssem.at[x], crsem.at[x], device_id=tile_at(o), device_id_type=MESH
                ).start()
            cre[x][len(CORNER_OFFS)] = cst[x][...]
        land[len(LINE_OFFS)] = stage[...]

    def receive(x, land, width, near):
        got = land.at[pl.ds(0, len(LINE_OFFS))]
        pltpu.make_async_copy(got, got, rsem.at[x]).wait()
        for k in range(4):
            near[k * width : (k + 1) * width, :] = land[line_slot[k], k ^ 1]
        back = (HALF - 1) - lanes(8, HALF)
        for b in range(0, 4 * width, 8):
            v = near[b : b + 8, :]
            turned = jnp.concatenate(
                [
                    jnp.take_along_axis(v[:, HALF:], back, axis=1),
                    jnp.take_along_axis(v[:, :HALF], back, axis=1),
                ],
                axis=1,
            )
            side = (lax.broadcasted_iota(jnp.int32, (8, TS), 0) + b) // width
            flag = jnp.where(
                side < 2, jnp.where(side == 0, flip[0], flip[1]), jnp.where(side == 2, flip[2], flip[3])
            )
            near[b : b + 8, :] = jnp.where(flag == 1, turned, v)

    def corners(x):
        got = cre[x].at[pl.ds(0, len(CORNER_OFFS))]
        pltpu.make_async_copy(got, got, crsem.at[x]).wait()
        values = {}
        for k in range(4):
            low = 4 if k < 2 else 0
            for e in range(2):
                slot, end, place = ghost[k, e]
                block = cre[x][slot]
                pair = jnp.where(end == 1, block[low : low + 2, :], block[low + 2 : low + 4, :])
                values[k, e] = jnp.where(place == 1, pair[:, HALF - 1 :], pair[:, :1])
        return values

    def advance(near, width, stage, s, ghosts, outer, terms):
        lane = lanes(1, TS)
        out = []
        for k in range(4):
            line = [near[k * width + j : k * width + j + 1, :] for j in range(2)]
            sums = []
            for j in range(2):
                low = jnp.where(lane < s, ghosts[k, 0][j : j + 1, :], pltpu.roll(line[j], s, 1))
                high = jnp.where(lane >= TS - s, ghosts[k, 1][j : j + 1, :], pltpu.roll(line[j], TS - s, 1))
                beyond = near[k * width + outer + j : k * width + outer + j + 1, :]
                sums.append(low + high + beyond + stage[k, j : j + 1, :])
            start0, start1, k00, k11, k01 = terms(k)
            out.append(
                [
                    KEEP * line[0] + start0 + (k00 * sums[0] + k01 * sums[1]),
                    KEEP * line[1] + start1 + (k01 * sums[0] + k11 * sums[1]),
                ]
            )
        return out

    def set_halo(v, s, lines):
        for j in range(2):
            for i in range(s):
                v[j, 7 - i : 8 - i, :] = lines[0][j]
                v[j, 264 + i : 265 + i, :] = lines[1][j]
                hs[j, i : i + 1, :] = lines[2][j]
                hs[j, HALF - 1 - i : HALF - i, :] = lines[3][j]
            hc[j] = jnp.transpose(hs[j])

    def plain_lines(near, width):
        return [[near[k * width + j : k * width + j + 1, :] for j in range(2)] for k in range(4)]

    def beside(v, j, r, s):
        lane = lanes(CHUNK, TS)
        here = v[j, pl.ds(r + 8, CHUNK), :]
        row = lax.broadcasted_iota(jnp.int32, (CHUNK, TS), 0)
        above = pltpu.roll(jnp.where(row >= CHUNK - s, v[j, pl.ds(r, CHUNK), :], here), s, 0)
        below = pltpu.roll(jnp.where(row < s, v[j, pl.ds(r + 16, CHUNK), :], here), CHUNK - s, 0)
        edge = hc[j, pl.ds(r, CHUNK), :]
        edge = jnp.concatenate([edge, edge], axis=1)
        west = jnp.where(lane < s, edge, pltpu.roll(here, s, 1))
        east = jnp.where(lane >= TS - s, edge, pltpu.roll(here, TS - s, 1))
        return here, (above + below) + (west + east)

    def put_edges(r, q, u, extra=()):
        lane = lanes(CHUNK, HALF)
        out = jnp.where(lane < 64, pltpu.roll(u[:, :HALF], 3, 1), pltpu.roll(u[:, HALF:], HALF - 3, 1))
        out = jnp.where(lane < 3, q[:, :HALF], jnp.where(lane >= HALF - 3, q[:, HALF:], out))
        for i, x in enumerate(extra):
            out = jnp.where(lane == 6 + i, pltpu.roll(x[:, :HALF], 6 + i, 1), out)
            out = jnp.where(lane == HALF - 7 - i, pltpu.roll(x[:, HALF:], HALF - 6 - i, 1), out)
        ec[pl.ds(r, CHUNK), :] = out

    def fill_stage(stage, v, s, second, terms):
        ect[...] = jnp.transpose(ec[...])
        for j in range(2):
            stage[0, j : j + 1, :] = v[j, 8:9, :]
            stage[1, j : j + 1, :] = v[j, 263:264, :]
            stage[2, j : j + 1, :] = ect[3 * j : 3 * j + 1, :]
            stage[3, j : j + 1, :] = ect[127 - 3 * j : 128 - 3 * j, :]
            if second is not None:
                b = second + j
                stage[0, b : b + 1, :] = v[j, 8 + s : 9 + s, :]
                stage[1, b : b + 1, :] = v[j, 263 - s : 264 - s, :]
                stage[2, b : b + 1, :] = ect[3 * j + s : 3 * j + s + 1, :]
                stage[3, b : b + 1, :] = ect[127 - 3 * j - s : 128 - 3 * j - s, :]
        if terms is not None:
            for i in range(3):
                stage[0, 2 + i : 3 + i, :] = terms[i, 0:1, :]
                stage[1, 2 + i : 3 + i, :] = terms[i, TS - 1 : TS, :]
                stage[2, 2 + i : 3 + i, :] = ect[6 + i : 7 + i, :]
                stage[3, 2 + i : 3 + i, :] = ect[121 - i : 122 - i, :]
            stage[:, 7:8, :] = jnp.zeros((4, 1, TS), jnp.float32)

    def over_chunks(step, first=0, count=CHUNKS):
        def body(i, carry):
            step(pl.multiple_of(first + i * CHUNK, CHUNK))
            return carry
        lax.fori_loop(0, count, body, 0)

    def sweep(src, start, terms, s, r):
        q, nq = beside(src, 0, r, s)
        u, nu = beside(src, 1, r, s)
        here = pl.ds(r, CHUNK)
        k00, k11, k01 = terms[0, here, :], terms[1, here, :], terms[2, here, :]
        q = KEEP * q + start[0, here, :] + (k00 * nq + k01 * nu)
        u = KEEP * u + start[1, here, :] + (k01 * nq + k11 * nu)
        return q, u

    def residual(src, r):
        here = pl.ds(r, CHUNK)
        q, nq = beside(src, 0, r, 1)
        u, nu = beside(src, 1, r, 1)
        w, cross, inv = wt[here, :], nc[here, :], iw[here, :]
        q0, u0 = q * inv, u * inv
        mq = rs[0, here, :] - (w * (CENTRE * q - nq) + nd[0, here, :] * q0 + cross * u0)
        mu = rs[1, here, :] - (w * (CENTRE * u - nu) + cross * q0 + nd[1, here, :] * u0)
        return mq, mu, q0, u0

    hs[...] = jnp.zeros_like(hs)
    for m in local + shared:
        m.wait()

    def start_fine(r):
        here = pl.ds(r, CHUNK)
        n0, n1, w = nd[0, here, :], nd[1, here, :], wt[here, :]
        cross = nc[here, :] * jnp.sqrt(n0 * n1)
        nc[here, :] = cross
        iw[here, :] = 1.0 / w
        q, u, k00, k11, k01 = smoother_terms(1.0, w, n0, n1, cross, rs[0, here, :], rs[1, here, :])
        kf[0, here, :], kf[1, here, :], kf[2, here, :] = k00, k11, k01
        sf[0, here, :], sf[1, here, :] = q, u
        va[0, pl.ds(r + 8, CHUNK), :], va[1, pl.ds(r + 8, CHUNK), :] = q, u
        put_edges(r, q, u, (k00, k11, k01))

    over_chunks(start_fine)
    fill_stage(st1, va, 1, 5, kf)
    send(0, st1, re1, 8)
    receive(0, re1, 8, nb1)
    set_halo(va, 1, plain_lines(nb1, 8))

    def first_sweep(r):
        q, u = sweep(va, sf, kf, 1, r)
        vb[0, pl.ds(r + 8, CHUNK), :], vb[1, pl.ds(r + 8, CHUNK), :] = q, u

    over_chunks(first_sweep)

    def terms_of(near):
        def terms(k):
            return [near[k * 8 + j : k * 8 + j + 1, :] for j in (0, 1, 2, 3, 4)]
        return terms

    set_halo(vb, 1, advance(nb1, 8, st1, 1, corners(0), 5, terms_of(nb1)))

    def start_coarse(r):
        here = pl.ds(r, CHUNK)
        mq, mu, _, _ = residual(vb, r)
        w = wt[here, :]
        cw = 0.25 * pair_sum(w)
        wiw[here, :] = w / cw
        q, u, k00, k11, k01 = smoother_terms(
            2.0, cw, pair_sum(nd[0, here, :]), pair_sum(nd[1, here, :]), pair_sum(nc[here, :]),
            pair_sum(mq), pair_sum(mu),
        )
        kc[0, here, :], kc[1, here, :], kc[2, here, :] = k00, k11, k01
        sc[0, here, :], sc[1, here, :] = q, u
        ca[0, pl.ds(r + 8, CHUNK), :], ca[1, pl.ds(r + 8, CHUNK), :] = q, u
        put_edges(r, q, u, (k00, k11, k01))

    over_chunks(start_coarse)
    fill_stage(st2, ca, 2, 5, kc)
    send(1, st2, re2, 8)
    receive(1, re2, 8, nb2)
    set_halo(ca, 2, plain_lines(nb2, 8))

    def coarse_sweep(r):
        q, u = sweep(ca, sc, kc, 2, r)
        cb[0, pl.ds(r + 8, CHUNK), :], cb[1, pl.ds(r + 8, CHUNK), :] = q, u

    over_chunks(coarse_sweep)
    set_halo(cb, 2, advance(nb2, 8, st2, 2, corners(1), 5, terms_of(nb2)))

    def correct(r):
        q, u = sweep(cb, sc, kc, 2, r)
        up = wiw[pl.ds(r, CHUNK), :]
        here = pl.ds(r + 8, CHUNK)
        q, u = vb[0, here, :] + up * q, vb[1, here, :] + up * u
        va[0, here, :], va[1, here, :] = q, u
        put_edges(r, q, u)

    over_chunks(correct)
    fill_stage(st3, va, 1, 2, None)
    send(2, st3, re3, 4)
    receive(2, re3, 4, nb3)
    set_halo(va, 1, plain_lines(nb3, 4))
    over_chunks(first_sweep)
    set_halo(vb, 1, advance(nb3, 4, st3, 1, corners(2), 2, terms_of(nb1)))

    def last_sweep(r):
        q, u = sweep(vb, sf, kf, 1, r)
        va[0, pl.ds(r + 8, CHUNK), :], va[1, pl.ds(r + 8, CHUNK), :] = q, u
        put_edges(r, q, u)

    over_chunks(last_sweep)
    fill_stage(st4, va, 1, None, None)
    send(3, st4, re4, 2)
    receive(3, re4, 2, nb4)
    set_halo(va, 1, plain_lines(nb4, 2))

    def finish(i, carry):
        r = pl.multiple_of(band + i * CHUNK, CHUNK)
        mq, mu, q, u = residual(va, r)
        here = pl.ds(pl.multiple_of(i * CHUNK, CHUNK), CHUNK)
        sol_out[0, here, :], sol_out[1, here, :] = q, u
        mis_out[0, here, :], mis_out[1, here, :] = mq, mu
        return carry

    lax.fori_loop(0, HALF // CHUNK, finish, 0)

    for x, land in enumerate((re1, re2, re3, re4)):
        sent = land.at[pl.ds(0, len(LINE_OFFS))]
        pltpu.make_async_copy(sent, sent, ssem.at[x]).wait()
        if x < 3:
            sent = cre[x].at[pl.ds(0, len(CORNER_OFFS))]
            pltpu.make_async_copy(sent, sent, cssem.at[x]).wait()


def body(right_side, pixel_weight, noise_diag, noise_corr, neighbours):
    f32 = jnp.float32
    vm = pltpu.VMEM
    plane, pair, triple, padded = (TS, TS), (2, TS, TS), (3, TS, TS), (2, TS + 16, TS)
    hbm = pl.BlockSpec(memory_space=pl.ANY)
    widths = (8, 8, 4, 2)
    dma = pltpu.SemaphoreType.DMA
    return pl.pallas_call(
        kernel,
        out_shape=[jax.ShapeDtypeStruct((2, HALF, TS), f32)] * 2,
        in_specs=[pl.BlockSpec(memory_space=pltpu.SMEM), hbm, hbm, hbm, hbm],
        out_specs=[pl.BlockSpec(memory_space=pltpu.VMEM)] * 2,
        scratch_shapes=[
            vm(pair, f32), vm(plane, f32), vm(pair, f32), vm(plane, f32), vm(plane, f32),
            vm(triple, f32), vm(triple, f32), vm(pair, f32), vm(pair, f32), vm(plane, f32),
            vm(padded, f32), vm(padded, f32), vm(padded, f32), vm(padded, f32),
            vm((TS, HALF), f32), vm((HALF, TS), f32), vm((2, HALF, TS), f32), vm((2, TS, HALF), f32),
        ]
        + [vm((4, n, TS), f32) for n in widths]
        + [vm((14, 4, n, TS), f32) for n in widths]
        + [vm((4 * n, TS), f32) for n in widths]
        + [
            *[vm((8, HALF), f32)] * 3, *[vm((26, 8, HALF), f32)] * 3,
            dma((6,)), dma((6,)), dma((6,)), dma((4,)), dma((4,)), dma((3,)), dma((3,)),
        ],
        compiler_params=pltpu.CompilerParams(
            collective_id=0, has_side_effects=True, vmem_limit_bytes=48 * 2**20
        ),
    )(neighbours, right_side, pixel_weight, noise_diag, noise_corr)


def solution(mesh):
    placed = (
        P(None, ("tile", "sub"), None),
        P(("tile", "sub"), None),
        P(None, ("tile", "sub"), None),
        P(("tile", "sub"), None),
        P(),
    )
    return jax.shard_map(
        body,
        mesh=mesh,
        in_specs=placed,
        out_specs=(P(None, ("tile", "sub"), None), P(None, ("tile", "sub"), None)),
        check_vma=False,
    )
```

```python
import functools

import jax
import jax.numpy as jnp
from jax import lax
from jax.experimental import pallas as pl
from jax.experimental.pallas import tpu as pltpu
from jax.sharding import PartitionSpec as P

MASS = 0.05
OMEGA = 0.8
KEEP = 1.0 - OMEGA
CENTRE = MASS + 4.0
TS = 256
HALF = 128
TILES = 128
CHUNK = 8
CHUNKS = TS // CHUNK
BATCH = 4
MESH = pl.DeviceIdType.MESH

LINE_OFFS = [-3, -2, -1, 1, 2, 3] + [64 + d for d in range(-3, 4)]
CORNER_OFFS = [-6, -5, -4, -3, -2, -1, 1, 2, 3, 4, 5, 6] + [64 + d for d in range(-6, 7)]


def slot_of(distance, reach):
    d = lax.rem(distance + TILES, TILES)
    far = d - (64 - reach) + 2 * reach
    near = jnp.where(d <= reach, d + reach - 1, d - (TILES - reach))
    slot = jnp.where((d <= reach) | (d >= TILES - reach), near, far)
    slot = jnp.where(d == 0, 4 * reach + 1, slot)
    return jnp.minimum(jnp.maximum(slot, 0), 4 * reach + 1)


def lanes(rows, cols):
    return lax.broadcasted_iota(jnp.int32, (rows, cols), 1)


def pair_sum(x):
    lane = lanes(CHUNK, TS)
    x = x + jnp.where(lane % 2 == 0, pltpu.roll(x, TS - 1, 1), pltpu.roll(x, 1, 1))
    row = lax.broadcasted_iota(jnp.int32, (CHUNK, TS), 0)
    return x + jnp.where(row % 2 == 0, pltpu.roll(x, CHUNK - 1, 0), pltpu.roll(x, 1, 0))


def smoother_terms(stiffness, w, n0, n1, cross, f0, f1):
    diag = (stiffness * CENTRE) * w * w
    b00, b11 = diag + n0, diag + n1
    scale = OMEGA / (b00 * b11 - cross * cross)
    k00, k11, k01 = scale * b11, scale * b00, -(scale * cross)
    v0 = w * (k00 * f0 + k01 * f1)
    v1 = w * (k01 * f0 + k11 * f1)
    ww = stiffness * w * w
    return v0, v1, ww * k00, ww * k11, ww * k01


def kernel(
    nb, rs_in, w_in, nd_in, nc_in, sol_out, mis_out,
    rs, wt, nd, nc, iw, kf, kc, sf, sc, wiw, va, vb, ca, cb,
    ec, ect, hs, hc, st1, st2, st3, st4, re1, re2, re3, re4, nb1, nb2, nb3, nb4,
    cs1, cs2, cs3, cr1, cr2, cr3, lsem, psem, prem, ssem, rsem, cssem, crsem,
):
    cst, cre = (cs1, cs2, cs3), (cr1, cr2, cr3)
    t = lax.axis_index("tile")
    c = lax.axis_index("sub")
    band = pl.multiple_of(c * HALF, HALF)

    def tile_at(offset):
        return (lax.rem(t + (offset + TILES), TILES), c)

    barrier = pltpu.get_barrier_semaphore()
    for o in CORNER_OFFS:
        pl.semaphore_signal(barrier, inc=1, device_id=tile_at(o), device_id_type=MESH)
    pl.semaphore_signal(barrier, inc=1, device_id=(t, 1 - c), device_id_type=MESH)

    rows = pl.ds(band, HALF)
    moves = [
        (rs_in.at[0], rs.at[0, rows]), (rs_in.at[1], rs.at[1, rows]), (w_in, wt.at[rows]),
        (nd_in.at[0], nd.at[0, rows]), (nd_in.at[1], nd.at[1, rows]), (nc_in, nc.at[rows]),
    ]
    local = [pltpu.make_async_copy(s, d, lsem.at[i]) for i, (s, d) in enumerate(moves)]
    for m in local:
        m.start()
    pl.semaphore_wait(barrier, len(CORNER_OFFS) + 1)
    shared = [
        pltpu.make_async_remote_copy(
            s, d, psem.at[i], prem.at[i], device_id=(t, 1 - c), device_id_type=MESH
        )
        for i, (s, d) in enumerate(moves)
    ]
    for m in shared:
        m.start()

    flip, line_slot, ghost = [], [], {}
    for k in range(4):
        n, f = nb[0, k, t], nb[2, k, t]
        flip.append(f)
        line_slot.append(slot_of(n - t, 3))
        base = 2 if k < 2 else 0
        for e in range(2):
            end = jnp.where(f == 1, 1 - e, e)
            q = base + end
            m, g = nb[0, q, n], nb[2, q, n]
            place = (k ^ 1) % 2
            ghost[k, e] = (slot_of(m - t, 6), end, jnp.where(g == 1, 1 - place, place))

    def send(x, stage, land, width):
        for o in LINE_OFFS:
            i = LINE_OFFS.index((-o + 3) % TILES - 3)
            pltpu.make_async_remote_copy(
                stage, land.at[i], ssem.at[x], rsem.at[x], device_id=tile_at(o), device_id_type=MESH
            ).start()
        if x < 3:
            lane = lanes(2, HALF)
            for k in range(4):
                pair = stage[k, 0:2, :]
                cst[x][2 * k : 2 * k + 2, :] = jnp.where(lane < 64, pair[:, :HALF], pair[:, HALF:])
            for o in CORNER_OFFS:
                i = CORNER_OFFS.index((-o + 6) % TILES - 6)
                pltpu.make_async_remote_copy(
                    cst[x], cre[x].at[i], cssem.at[x], crsem.at[x], device_id=tile_at(o), device_id_type=MESH
                ).start()
            cre[x][len(CORNER_OFFS)] = cst[x][...]
        land[len(LINE_OFFS)] = stage[...]

    def receive(x, land, width, near):
        got = land.at[pl.ds(0, len(LINE_OFFS))]
        pltpu.make_async_copy(got, got, rsem.at[x]).wait()
        for k in range(4):
            near[k * width : (k + 1) * width, :] = land[line_slot[k], k ^ 1]
        back = (HALF - 1) - lanes(8, HALF)
        for b in range(0, 4 * width, 8):
            v = near[b : b + 8, :]
            turned = jnp.concatenate(
                [
                    jnp.take_along_axis(v[:, HALF:], back, axis=1),
                    jnp.take_along_axis(v[:, :HALF], back, axis=1),
                ],
                axis=1,
            )
            side = (lax.broadcasted_iota(jnp.int32, (8, TS), 0) + b) // width
            flag = jnp.where(
                side < 2, jnp.where(side == 0, flip[0], flip[1]), jnp.where(side == 2, flip[2], flip[3])
            )
            near[b : b + 8, :] = jnp.where(flag == 1, turned, v)

    def corners(x):
        got = cre[x].at[pl.ds(0, len(CORNER_OFFS))]
        pltpu.make_async_copy(got, got, crsem.at[x]).wait()
        values = {}
        for k in range(4):
            low = 4 if k < 2 else 0
            for e in range(2):
                slot, end, place = ghost[k, e]
                block = cre[x][slot]
                pair = jnp.where(end == 1, block[low : low + 2, :], block[low + 2 : low + 4, :])
                values[k, e] = jnp.where(place == 1, pair[:, HALF - 1 :], pair[:, :1])
        return values

    def advance(near, width, stage, s, ghosts, outer, terms):
        lane = lanes(1, TS)
        out = []
        for k in range(4):
            line = [near[k * width + j : k * width + j + 1, :] for j in range(2)]
            sums = []
            for j in range(2):
                low = jnp.where(lane < s, ghosts[k, 0][j : j + 1, :], pltpu.roll(line[j], s, 1))
                high = jnp.where(lane >= TS - s, ghosts[k, 1][j : j + 1, :], pltpu.roll(line[j], TS - s, 1))
                beyond = near[k * width + outer + j : k * width + outer + j + 1, :]
                sums.append(low + high + beyond + stage[k, j : j + 1, :])
            start0, start1, k00, k11, k01 = terms(k)
            out.append(
                [
                    KEEP * line[0] + start0 + (k00 * sums[0] + k01 * sums[1]),
                    KEEP * line[1] + start1 + (k01 * sums[0] + k11 * sums[1]),
                ]
            )
        return out

    def set_halo(v, s, lines):
        for j in range(2):
            for i in range(s):
                v[j, 7 - i : 8 - i, :] = lines[0][j]
                v[j, 264 + i : 265 + i, :] = lines[1][j]
                hs[j, i : i + 1, :] = lines[2][j]
                hs[j, HALF - 1 - i : HALF - i, :] = lines[3][j]
            hc[j] = jnp.transpose(hs[j])

    def plain_lines(near, width):
        return [[near[k * width + j : k * width + j + 1, :] for j in range(2)] for k in range(4)]

    def beside(v, j, r, s):
        lane = lanes(CHUNK, TS)
        here = v[j, pl.ds(r + 8, CHUNK), :]
        row = lax.broadcasted_iota(jnp.int32, (CHUNK, TS), 0)
        above = pltpu.roll(jnp.where(row >= CHUNK - s, v[j, pl.ds(r, CHUNK), :], here), s, 0)
        below = pltpu.roll(jnp.where(row < s, v[j, pl.ds(r + 16, CHUNK), :], here), CHUNK - s, 0)
        edge = hc[j, pl.ds(r, CHUNK), :]
        edge = jnp.concatenate([edge, edge], axis=1)
        west = jnp.where(lane < s, edge, pltpu.roll(here, s, 1))
        east = jnp.where(lane >= TS - s, edge, pltpu.roll(here, TS - s, 1))
        return here, (above + below) + (west + east)

    def put_edges(r, q, u, extra=()):
        lane = lanes(CHUNK, HALF)
        out = jnp.where(lane < 64, pltpu.roll(u[:, :HALF], 3, 1), pltpu.roll(u[:, HALF:], HALF - 3, 1))
        out = jnp.where(lane < 3, q[:, :HALF], jnp.where(lane >= HALF - 3, q[:, HALF:], out))
        for i, x in enumerate(extra):
            out = jnp.where(lane == 6 + i, pltpu.roll(x[:, :HALF], 6 + i, 1), out)
            out = jnp.where(lane == HALF - 7 - i, pltpu.roll(x[:, HALF:], HALF - 6 - i, 1), out)
        ec[pl.ds(r, CHUNK), :] = out

    def fill_stage(stage, v, s, second, terms):
        ect[...] = jnp.transpose(ec[...])
        for j in range(2):
            stage[0, j : j + 1, :] = v[j, 8:9, :]
            stage[1, j : j + 1, :] = v[j, 263:264, :]
            stage[2, j : j + 1, :] = ect[3 * j : 3 * j + 1, :]
            stage[3, j : j + 1, :] = ect[127 - 3 * j : 128 - 3 * j, :]
            if second is not None:
                b = second + j
                stage[0, b : b + 1, :] = v[j, 8 + s : 9 + s, :]
                stage[1, b : b + 1, :] = v[j, 263 - s : 264 - s, :]
                stage[2, b : b + 1, :] = ect[3 * j + s : 3 * j + s + 1, :]
                stage[3, b : b + 1, :] = ect[127 - 3 * j - s : 128 - 3 * j - s, :]
        if terms is not None:
            for i in range(3):
                stage[0, 2 + i : 3 + i, :] = terms[i, 0:1, :]
                stage[1, 2 + i : 3 + i, :] = terms[i, TS - 1 : TS, :]
                stage[2, 2 + i : 3 + i, :] = ect[6 + i : 7 + i, :]
                stage[3, 2 + i : 3 + i, :] = ect[121 - i : 122 - i, :]
            stage[:, 7:8, :] = jnp.zeros((4, 1, TS), jnp.float32)

    def over_chunks(step, first=0, count=CHUNKS):
        def body(i, carry):
            for b in range(BATCH):
                step(pl.multiple_of(first + (i * BATCH + b) * CHUNK, CHUNK))
            return carry
        lax.fori_loop(0, count // BATCH, body, 0)

    def sweep(src, start, terms, s, r):
        q, nq = beside(src, 0, r, s)
        u, nu = beside(src, 1, r, s)
        here = pl.ds(r, CHUNK)
        k00, k11, k01 = terms[0, here, :], terms[1, here, :], terms[2, here, :]
        q = KEEP * q + start[0, here, :] + (k00 * nq + k01 * nu)
        u = KEEP * u + start[1, here, :] + (k01 * nq + k11 * nu)
        return q, u

    def residual(src, r):
        here = pl.ds(r, CHUNK)
        q, nq = beside(src, 0, r, 1)
        u, nu = beside(src, 1, r, 1)
        w, cross, inv = wt[here, :], nc[here, :], iw[here, :]
        q0, u0 = q * inv, u * inv
        mq = rs[0, here, :] - (w * (CENTRE * q - nq) + nd[0, here, :] * q0 + cross * u0)
        mu = rs[1, here, :] - (w * (CENTRE * u - nu) + cross * q0 + nd[1, here, :] * u0)
        return mq, mu, q0, u0

    hs[...] = jnp.zeros_like(hs)
    for m in local + shared:
        m.wait()

    def start_fine(r):
        here = pl.ds(r, CHUNK)
        n0, n1, w = nd[0, here, :], nd[1, here, :], wt[here, :]
        cross = nc[here, :] * jnp.sqrt(n0 * n1)
        nc[here, :] = cross
        iw[here, :] = 1.0 / w
        q, u, k00, k11, k01 = smoother_terms(1.0, w, n0, n1, cross, rs[0, here, :], rs[1, here, :])
        kf[0, here, :], kf[1, here, :], kf[2, here, :] = k00, k11, k01
        sf[0, here, :], sf[1, here, :] = q, u
        va[0, pl.ds(r + 8, CHUNK), :], va[1, pl.ds(r + 8, CHUNK), :] = q, u
        put_edges(r, q, u, (k00, k11, k01))

    over_chunks(start_fine)
    fill_stage(st1, va, 1, 5, kf)
    send(0, st1, re1, 8)
    receive(0, re1, 8, nb1)
    set_halo(va, 1, plain_lines(nb1, 8))

    def first_sweep(r):
        q, u = sweep(va, sf, kf, 1, r)
        vb[0, pl.ds(r + 8, CHUNK), :], vb[1, pl.ds(r + 8, CHUNK), :] = q, u

    over_chunks(first_sweep)

    def terms_of(near):
        def terms(k):
            return [near[k * 8 + j : k * 8 + j + 1, :] for j in (0, 1, 2, 3, 4)]
        return terms

    set_halo(vb, 1, advance(nb1, 8, st1, 1, corners(0), 5, terms_of(nb1)))

    def start_coarse(r):
        here = pl.ds(r, CHUNK)
        mq, mu, _, _ = residual(vb, r)
        w = wt[here, :]
        cw = 0.25 * pair_sum(w)
        wiw[here, :] = w / cw
        q, u, k00, k11, k01 = smoother_terms(
            2.0, cw, pair_sum(nd[0, here, :]), pair_sum(nd[1, here, :]), pair_sum(nc[here, :]),
            pair_sum(mq), pair_sum(mu),
        )
        kc[0, here, :], kc[1, here, :], kc[2, here, :] = k00, k11, k01
        sc[0, here, :], sc[1, here, :] = q, u
        ca[0, pl.ds(r + 8, CHUNK), :], ca[1, pl.ds(r + 8, CHUNK), :] = q, u
        put_edges(r, q, u, (k00, k11, k01))

    over_chunks(start_coarse)
    fill_stage(st2, ca, 2, 5, kc)
    send(1, st2, re2, 8)
    receive(1, re2, 8, nb2)
    set_halo(ca, 2, plain_lines(nb2, 8))

    def coarse_sweep(r):
        q, u = sweep(ca, sc, kc, 2, r)
        cb[0, pl.ds(r + 8, CHUNK), :], cb[1, pl.ds(r + 8, CHUNK), :] = q, u

    over_chunks(coarse_sweep)
    set_halo(cb, 2, advance(nb2, 8, st2, 2, corners(1), 5, terms_of(nb2)))

    def correct(r):
        q, u = sweep(cb, sc, kc, 2, r)
        up = wiw[pl.ds(r, CHUNK), :]
        here = pl.ds(r + 8, CHUNK)
        q, u = vb[0, here, :] + up * q, vb[1, here, :] + up * u
        va[0, here, :], va[1, here, :] = q, u
        put_edges(r, q, u)

    over_chunks(correct)
    fill_stage(st3, va, 1, 2, None)
    send(2, st3, re3, 4)
    receive(2, re3, 4, nb3)
    set_halo(va, 1, plain_lines(nb3, 4))
    over_chunks(first_sweep)
    set_halo(vb, 1, advance(nb3, 4, st3, 1, corners(2), 2, terms_of(nb1)))

    def last_sweep(r):
        q, u = sweep(vb, sf, kf, 1, r)
        va[0, pl.ds(r + 8, CHUNK), :], va[1, pl.ds(r + 8, CHUNK), :] = q, u
        put_edges(r, q, u)

    over_chunks(last_sweep)
    fill_stage(st4, va, 1, None, None)
    send(3, st4, re4, 2)
    receive(3, re4, 2, nb4)
    set_halo(va, 1, plain_lines(nb4, 2))

    def finish(i):
        r = pl.multiple_of(band + i, CHUNK)
        mq, mu, q, u = residual(va, r)
        here = pl.ds(i, CHUNK)
        sol_out[0, here, :], sol_out[1, here, :] = q, u
        mis_out[0, here, :], mis_out[1, here, :] = mq, mu

    over_chunks(finish, 0, HALF // CHUNK)

    for x, land in enumerate((re1, re2, re3, re4)):
        sent = land.at[pl.ds(0, len(LINE_OFFS))]
        pltpu.make_async_copy(sent, sent, ssem.at[x]).wait()
        if x < 3:
            sent = cre[x].at[pl.ds(0, len(CORNER_OFFS))]
            pltpu.make_async_copy(sent, sent, cssem.at[x]).wait()


def body(right_side, pixel_weight, noise_diag, noise_corr, neighbours):
    f32 = jnp.float32
    vm = pltpu.VMEM
    plane, pair, triple, padded = (TS, TS), (2, TS, TS), (3, TS, TS), (2, TS + 16, TS)
    hbm = pl.BlockSpec(memory_space=pl.ANY)
    widths = (8, 8, 4, 2)
    dma = pltpu.SemaphoreType.DMA
    return pl.pallas_call(
        kernel,
        out_shape=[jax.ShapeDtypeStruct((2, HALF, TS), f32)] * 2,
        in_specs=[pl.BlockSpec(memory_space=pltpu.SMEM), hbm, hbm, hbm, hbm],
        out_specs=[pl.BlockSpec(memory_space=pltpu.VMEM)] * 2,
        scratch_shapes=[
            vm(pair, f32), vm(plane, f32), vm(pair, f32), vm(plane, f32), vm(plane, f32),
            vm(triple, f32), vm(triple, f32), vm(pair, f32), vm(pair, f32), vm(plane, f32),
            vm(padded, f32), vm(padded, f32), vm(padded, f32), vm(padded, f32),
            vm((TS, HALF), f32), vm((HALF, TS), f32), vm((2, HALF, TS), f32), vm((2, TS, HALF), f32),
        ]
        + [vm((4, n, TS), f32) for n in widths]
        + [vm((14, 4, n, TS), f32) for n in widths]
        + [vm((4 * n, TS), f32) for n in widths]
        + [
            *[vm((8, HALF), f32)] * 3, *[vm((26, 8, HALF), f32)] * 3,
            dma((6,)), dma((6,)), dma((6,)), dma((4,)), dma((4,)), dma((3,)), dma((3,)),
        ],
        compiler_params=pltpu.CompilerParams(
            collective_id=0, has_side_effects=True, vmem_limit_bytes=48 * 2**20
        ),
    )(neighbours, right_side, pixel_weight, noise_diag, noise_corr)


def solution(mesh):
    placed = (
        P(None, ("tile", "sub"), None),
        P(("tile", "sub"), None),
        P(None, ("tile", "sub"), None),
        P(("tile", "sub"), None),
        P(),
    )
    return jax.shard_map(
        body,
        mesh=mesh,
        in_specs=placed,
        out_specs=(P(None, ("tile", "sub"), None), P(None, ("tile", "sub"), None)),
        check_vma=False,
    )
```

```python
import functools

import jax
import jax.numpy as jnp
from jax import lax
from jax.experimental import pallas as pl
from jax.experimental.pallas import tpu as pltpu
from jax.sharding import PartitionSpec as P

MASS = 0.05
OMEGA = 0.8
KEEP = 1.0 - OMEGA
CENTRE = MASS + 4.0
TS = 256
HALF = 128
TILES = 128
CHUNK = 8
CHUNKS = TS // CHUNK
BATCH = 4
MESH = pl.DeviceIdType.MESH

LINE_OFFS = [-3, -2, -1, 1, 2, 3] + [64 + d for d in range(-3, 4)]
CORNER_OFFS = [-6, -5, -4, -3, -2, -1, 1, 2, 3, 4, 5, 6] + [64 + d for d in range(-6, 7)]


def slot_of(distance, reach):
    d = lax.rem(distance + TILES, TILES)
    far = d - (64 - reach) + 2 * reach
    near = jnp.where(d <= reach, d + reach - 1, d - (TILES - reach))
    slot = jnp.where((d <= reach) | (d >= TILES - reach), near, far)
    slot = jnp.where(d == 0, 4 * reach + 1, slot)
    return jnp.minimum(jnp.maximum(slot, 0), 4 * reach + 1)


def lanes(rows, cols):
    return lax.broadcasted_iota(jnp.int32, (rows, cols), 1)


def pair_sum(x):
    lane = lanes(CHUNK, TS)
    x = x + jnp.where(lane % 2 == 0, pltpu.roll(x, TS - 1, 1), pltpu.roll(x, 1, 1))
    row = lax.broadcasted_iota(jnp.int32, (CHUNK, TS), 0)
    return x + jnp.where(row % 2 == 0, pltpu.roll(x, CHUNK - 1, 0), pltpu.roll(x, 1, 0))


def smoother_terms(stiffness, w, n0, n1, cross, f0, f1):
    diag = (stiffness * CENTRE) * w * w
    b00, b11 = diag + n0, diag + n1
    scale = OMEGA / (b00 * b11 - cross * cross)
    k00, k11, k01 = scale * b11, scale * b00, -(scale * cross)
    v0 = w * (k00 * f0 + k01 * f1)
    v1 = w * (k01 * f0 + k11 * f1)
    ww = stiffness * w * w
    return v0, v1, ww * k00, ww * k11, ww * k01


def kernel(
    nb, rs_in, w_in, nd_in, nc_in, sol_out, mis_out,
    rs, wt, nd, nc, iw, kf, kc, sf, sc, wiw, va, vb, ca, cb,
    ec, ect, hs, hc, st1, st2, st3, st4, re1, re2, re3, re4, nb1, nb2, nb3, nb4,
    cs1, cs2, cs3, cr1, cr2, cr3, mo1, mo2, mo3, mr1, mr2, mr3, nm1, nm2, nm3,
    lsem, psem, prem, ssem, rsem, cssem, crsem, msem, mrsem,
):
    cst, cre = (cs1, cs2, cs3), (cr1, cr2, cr3)
    t = lax.axis_index("tile")
    c = lax.axis_index("sub")
    band = pl.multiple_of(c * HALF, HALF)

    def tile_at(offset):
        return (lax.rem(t + (offset + TILES), TILES), c)

    barrier = pltpu.get_barrier_semaphore()
    for o in CORNER_OFFS:
        pl.semaphore_signal(barrier, inc=1, device_id=tile_at(o), device_id_type=MESH)
    pl.semaphore_signal(barrier, inc=1, device_id=(t, 1 - c), device_id_type=MESH)

    rows = pl.ds(band, HALF)
    moves = [
        (rs_in.at[0], rs.at[0, rows]), (rs_in.at[1], rs.at[1, rows]), (w_in, wt.at[rows]),
        (nd_in.at[0], nd.at[0, rows]), (nd_in.at[1], nd.at[1, rows]), (nc_in, nc.at[rows]),
    ]
    local = [pltpu.make_async_copy(s, d, lsem.at[i]) for i, (s, d) in enumerate(moves)]
    for m in local:
        m.start()
    pl.semaphore_wait(barrier, len(CORNER_OFFS) + 1)
    shared = [
        pltpu.make_async_remote_copy(
            s, d, psem.at[i], prem.at[i], device_id=(t, 1 - c), device_id_type=MESH
        )
        for i, (s, d) in enumerate(moves)
    ]
    for m in shared:
        m.start()

    flip, line_slot, ghost = [], [], {}
    for k in range(4):
        n, f = nb[0, k, t], nb[2, k, t]
        flip.append(f)
        line_slot.append(slot_of(n - t, 3))
        base = 2 if k < 2 else 0
        for e in range(2):
            end = jnp.where(f == 1, 1 - e, e)
            q = base + end
            m, g = nb[0, q, n], nb[2, q, n]
            place = (k ^ 1) % 2
            ghost[k, e] = (slot_of(m - t, 6), end, jnp.where(g == 1, 1 - place, place))

    def spread(stage, land, gone, come):
        for o in LINE_OFFS:
            i = LINE_OFFS.index((-o + 3) % TILES - 3)
            pltpu.make_async_remote_copy(
                stage, land.at[i], gone, come, device_id=tile_at(o), device_id_type=MESH
            ).start()

    def send(x, stage, land):
        spread(stage, land, ssem.at[x], rsem.at[x])
        land[len(LINE_OFFS)] = stage[...]

    def send_more(x, stage, more, land):
        lane = lanes(2, HALF)
        for k in range(4):
            pair = stage[k, 0:2, :]
            cst[x][2 * k : 2 * k + 2, :] = jnp.where(lane < 64, pair[:, :HALF], pair[:, HALF:])
        for o in CORNER_OFFS:
            i = CORNER_OFFS.index((-o + 6) % TILES - 6)
            pltpu.make_async_remote_copy(
                cst[x], cre[x].at[i], cssem.at[x], crsem.at[x], device_id=tile_at(o), device_id_type=MESH
            ).start()
        spread(more, land, msem.at[x], mrsem.at[x])
        cre[x][len(CORNER_OFFS)] = cst[x][...]
        land[len(LINE_OFFS)] = more[...]

    def receive(come, land, width, near):
        got = land.at[pl.ds(0, len(LINE_OFFS))]
        pltpu.make_async_copy(got, got, come).wait()
        for k in range(4):
            near[k * width : (k + 1) * width, :] = land[line_slot[k], k ^ 1]
        back = (HALF - 1) - lanes(8, HALF)
        for b in range(0, 4 * width, 8):
            v = near[b : b + 8, :]
            turned = jnp.concatenate(
                [
                    jnp.take_along_axis(v[:, HALF:], back, axis=1),
                    jnp.take_along_axis(v[:, :HALF], back, axis=1),
                ],
                axis=1,
            )
            side = (lax.broadcasted_iota(jnp.int32, (8, TS), 0) + b) // width
            flag = jnp.where(
                side < 2, jnp.where(side == 0, flip[0], flip[1]), jnp.where(side == 2, flip[2], flip[3])
            )
            near[b : b + 8, :] = jnp.where(flag == 1, turned, v)

    def corners(x):
        got = cre[x].at[pl.ds(0, len(CORNER_OFFS))]
        pltpu.make_async_copy(got, got, crsem.at[x]).wait()
        values = {}
        for k in range(4):
            low = 4 if k < 2 else 0
            for e in range(2):
                slot, end, place = ghost[k, e]
                block = cre[x][slot]
                pair = jnp.where(end == 1, block[low : low + 2, :], block[low + 2 : low + 4, :])
                values[k, e] = jnp.where(place == 1, pair[:, HALF - 1 :], pair[:, :1])
        return values

    def advance(near, more, width, stage, s, ghosts, terms):
        lane = lanes(1, TS)
        out = []
        for k in range(4):
            line = [near[2 * k + j : 2 * k + j + 1, :] for j in range(2)]
            sums = []
            for j in range(2):
                low = jnp.where(lane < s, ghosts[k, 0][j : j + 1, :], pltpu.roll(line[j], s, 1))
                high = jnp.where(lane >= TS - s, ghosts[k, 1][j : j + 1, :], pltpu.roll(line[j], TS - s, 1))
                beyond = more[k * width + j : k * width + j + 1, :]
                sums.append(low + high + beyond + stage[k, j : j + 1, :])
            start0, start1, k00, k11, k01 = terms(k)
            out.append(
                [
                    KEEP * line[0] + start0 + (k00 * sums[0] + k01 * sums[1]),
                    KEEP * line[1] + start1 + (k01 * sums[0] + k11 * sums[1]),
                ]
            )
        return out

    def set_halo(v, s, lines):
        for j in range(2):
            for i in range(s):
                v[j, 7 - i : 8 - i, :] = lines[0][j]
                v[j, 264 + i : 265 + i, :] = lines[1][j]
                hs[j, i : i + 1, :] = lines[2][j]
                hs[j, HALF - 1 - i : HALF - i, :] = lines[3][j]
            hc[j] = jnp.transpose(hs[j])

    def plain_lines(near):
        return [[near[2 * k + j : 2 * k + j + 1, :] for j in range(2)] for k in range(4)]

    def beside(v, j, r, s):
        lane = lanes(CHUNK, TS)
        here = v[j, pl.ds(r + 8, CHUNK), :]
        row = lax.broadcasted_iota(jnp.int32, (CHUNK, TS), 0)
        above = pltpu.roll(jnp.where(row >= CHUNK - s, v[j, pl.ds(r, CHUNK), :], here), s, 0)
        below = pltpu.roll(jnp.where(row < s, v[j, pl.ds(r + 16, CHUNK), :], here), CHUNK - s, 0)
        edge = hc[j, pl.ds(r, CHUNK), :]
        edge = jnp.concatenate([edge, edge], axis=1)
        west = jnp.where(lane < s, edge, pltpu.roll(here, s, 1))
        east = jnp.where(lane >= TS - s, edge, pltpu.roll(here, TS - s, 1))
        return here, (above + below) + (west + east)

    def put_edges(r, q, u, extra=()):
        lane = lanes(CHUNK, HALF)
        out = jnp.where(lane < 64, pltpu.roll(u[:, :HALF], 3, 1), pltpu.roll(u[:, HALF:], HALF - 3, 1))
        out = jnp.where(lane < 3, q[:, :HALF], jnp.where(lane >= HALF - 3, q[:, HALF:], out))
        for i, x in enumerate(extra):
            out = jnp.where(lane == 6 + i, pltpu.roll(x[:, :HALF], 6 + i, 1), out)
            out = jnp.where(lane == HALF - 7 - i, pltpu.roll(x[:, HALF:], HALF - 6 - i, 1), out)
        ec[pl.ds(r, CHUNK), :] = out

    def fill_stage(stage, v):
        ect[...] = jnp.transpose(ec[...])
        for j in range(2):
            stage[0, j : j + 1, :] = v[j, 8:9, :]
            stage[1, j : j + 1, :] = v[j, 263:264, :]
            stage[2, j : j + 1, :] = ect[3 * j : 3 * j + 1, :]
            stage[3, j : j + 1, :] = ect[127 - 3 * j : 128 - 3 * j, :]

    def fill_more(more, v, s, terms):
        for j in range(2):
            more[0, j : j + 1, :] = v[j, 8 + s : 9 + s, :]
            more[1, j : j + 1, :] = v[j, 263 - s : 264 - s, :]
            more[2, j : j + 1, :] = ect[3 * j + s : 3 * j + s + 1, :]
            more[3, j : j + 1, :] = ect[127 - 3 * j - s : 128 - 3 * j - s, :]
        if terms is not None:
            for i in range(3):
                more[0, 2 + i : 3 + i, :] = terms[i, 0:1, :]
                more[1, 2 + i : 3 + i, :] = terms[i, TS - 1 : TS, :]
                more[2, 2 + i : 3 + i, :] = ect[6 + i : 7 + i, :]
                more[3, 2 + i : 3 + i, :] = ect[121 - i : 122 - i, :]
            more[:, 5:6, :] = jnp.zeros((4, 1, TS), jnp.float32)

    def over_chunks(step, first=0, count=CHUNKS):
        def body(i, carry):
            for b in range(BATCH):
                step(pl.multiple_of(first + (i * BATCH + b) * CHUNK, CHUNK))
            return carry
        lax.fori_loop(0, count // BATCH, body, 0)

    def sweep(src, start, terms, s, r):
        q, nq = beside(src, 0, r, s)
        u, nu = beside(src, 1, r, s)
        here = pl.ds(r, CHUNK)
        k00, k11, k01 = terms[0, here, :], terms[1, here, :], terms[2, here, :]
        q = KEEP * q + start[0, here, :] + (k00 * nq + k01 * nu)
        u = KEEP * u + start[1, here, :] + (k01 * nq + k11 * nu)
        return q, u

    def residual(src, r):
        here = pl.ds(r, CHUNK)
        q, nq = beside(src, 0, r, 1)
        u, nu = beside(src, 1, r, 1)
        w, cross, inv = wt[here, :], nc[here, :], iw[here, :]
        q0, u0 = q * inv, u * inv
        mq = rs[0, here, :] - (w * (CENTRE * q - nq) + nd[0, here, :] * q0 + cross * u0)
        mu = rs[1, here, :] - (w * (CENTRE * u - nu) + cross * q0 + nd[1, here, :] * u0)
        return mq, mu, q0, u0

    hs[...] = jnp.zeros_like(hs)
    for m in local + shared:
        m.wait()

    def start_fine(r):
        here = pl.ds(r, CHUNK)
        n0, n1, w = nd[0, here, :], nd[1, here, :], wt[here, :]
        cross = nc[here, :] * jnp.sqrt(n0 * n1)
        nc[here, :] = cross
        iw[here, :] = 1.0 / w
        q, u, k00, k11, k01 = smoother_terms(1.0, w, n0, n1, cross, rs[0, here, :], rs[1, here, :])
        kf[0, here, :], kf[1, here, :], kf[2, here, :] = k00, k11, k01
        sf[0, here, :], sf[1, here, :] = q, u
        va[0, pl.ds(r + 8, CHUNK), :], va[1, pl.ds(r + 8, CHUNK), :] = q, u
        put_edges(r, q, u, (k00, k11, k01))

    over_chunks(start_fine)
    fill_stage(st1, va)
    send(0, st1, re1)
    fill_more(mo1, va, 1, kf)
    send_more(0, st1, mo1, mr1)
    receive(rsem.at[0], re1, 2, nb1)
    set_halo(va, 1, plain_lines(nb1))

    def first_sweep(r):
        q, u = sweep(va, sf, kf, 1, r)
        vb[0, pl.ds(r + 8, CHUNK), :], vb[1, pl.ds(r + 8, CHUNK), :] = q, u

    over_chunks(first_sweep)

    def terms_of(near, more):
        def terms(k):
            starts = [near[2 * k + j : 2 * k + j + 1, :] for j in range(2)]
            return starts + [more[6 * k + j : 6 * k + j + 1, :] for j in (2, 3, 4)]
        return terms

    receive(mrsem.at[0], mr1, 6, nm1)
    set_halo(vb, 1, advance(nb1, nm1, 6, st1, 1, corners(0), terms_of(nb1, nm1)))

    def start_coarse(r):
        here = pl.ds(r, CHUNK)
        mq, mu, _, _ = residual(vb, r)
        w = wt[here, :]
        cw = 0.25 * pair_sum(w)
        wiw[here, :] = w / cw
        q, u, k00, k11, k01 = smoother_terms(
            2.0, cw, pair_sum(nd[0, here, :]), pair_sum(nd[1, here, :]), pair_sum(nc[here, :]),
            pair_sum(mq), pair_sum(mu),
        )
        kc[0, here, :], kc[1, here, :], kc[2, here, :] = k00, k11, k01
        sc[0, here, :], sc[1, here, :] = q, u
        ca[0, pl.ds(r + 8, CHUNK), :], ca[1, pl.ds(r + 8, CHUNK), :] = q, u
        put_edges(r, q, u, (k00, k11, k01))

    over_chunks(start_coarse)
    fill_stage(st2, ca)
    send(1, st2, re2)
    fill_more(mo2, ca, 2, kc)
    send_more(1, st2, mo2, mr2)
    receive(rsem.at[1], re2, 2, nb2)
    set_halo(ca, 2, plain_lines(nb2))

    def coarse_sweep(r):
        q, u = sweep(ca, sc, kc, 2, r)
        cb[0, pl.ds(r + 8, CHUNK), :], cb[1, pl.ds(r + 8, CHUNK), :] = q, u

    over_chunks(coarse_sweep)
    receive(mrsem.at[1], mr2, 6, nm2)
    set_halo(cb, 2, advance(nb2, nm2, 6, st2, 2, corners(1), terms_of(nb2, nm2)))

    def correct(r):
        q, u = sweep(cb, sc, kc, 2, r)
        up = wiw[pl.ds(r, CHUNK), :]
        here = pl.ds(r + 8, CHUNK)
        q, u = vb[0, here, :] + up * q, vb[1, here, :] + up * u
        va[0, here, :], va[1, here, :] = q, u
        put_edges(r, q, u)

    over_chunks(correct)
    fill_stage(st3, va)
    send(2, st3, re3)
    fill_more(mo3, va, 1, None)
    send_more(2, st3, mo3, mr3)
    receive(rsem.at[2], re3, 2, nb3)
    set_halo(va, 1, plain_lines(nb3))
    over_chunks(first_sweep)
    receive(mrsem.at[2], mr3, 2, nm3)
    set_halo(vb, 1, advance(nb3, nm3, 2, st3, 1, corners(2), terms_of(nb1, nm1)))

    def last_sweep(r):
        q, u = sweep(vb, sf, kf, 1, r)
        va[0, pl.ds(r + 8, CHUNK), :], va[1, pl.ds(r + 8, CHUNK), :] = q, u
        put_edges(r, q, u)

    over_chunks(last_sweep)
    fill_stage(st4, va)
    send(3, st4, re4)
    receive(rsem.at[3], re4, 2, nb4)
    set_halo(va, 1, plain_lines(nb4))

    def finish(i):
        r = pl.multiple_of(band + i, CHUNK)
        mq, mu, q, u = residual(va, r)
        here = pl.ds(i, CHUNK)
        sol_out[0, here, :], sol_out[1, here, :] = q, u
        mis_out[0, here, :], mis_out[1, here, :] = mq, mu

    over_chunks(finish, 0, HALF // CHUNK)

    for x, land in enumerate((re1, re2, re3, re4)):
        sent = land.at[pl.ds(0, len(LINE_OFFS))]
        pltpu.make_async_copy(sent, sent, ssem.at[x]).wait()
        if x < 3:
            sent = cre[x].at[pl.ds(0, len(CORNER_OFFS))]
            pltpu.make_async_copy(sent, sent, cssem.at[x]).wait()
            sent = (mr1, mr2, mr3)[x].at[pl.ds(0, len(LINE_OFFS))]
            pltpu.make_async_copy(sent, sent, msem.at[x]).wait()


def body(right_side, pixel_weight, noise_diag, noise_corr, neighbours):
    f32 = jnp.float32
    vm = pltpu.VMEM
    plane, pair, triple, padded = (TS, TS), (2, TS, TS), (3, TS, TS), (2, TS + 16, TS)
    hbm = pl.BlockSpec(memory_space=pl.ANY)
    widths, later = (2, 2, 2, 2), (6, 6, 2)
    dma = pltpu.SemaphoreType.DMA
    return pl.pallas_call(
        kernel,
        out_shape=[jax.ShapeDtypeStruct((2, HALF, TS), f32)] * 2,
        in_specs=[pl.BlockSpec(memory_space=pltpu.SMEM), hbm, hbm, hbm, hbm],
        out_specs=[pl.BlockSpec(memory_space=pltpu.VMEM)] * 2,
        scratch_shapes=[
            vm(pair, f32), vm(plane, f32), vm(pair, f32), vm(plane, f32), vm(plane, f32),
            vm(triple, f32), vm(triple, f32), vm(pair, f32), vm(pair, f32), vm(plane, f32),
            vm(padded, f32), vm(padded, f32), vm(padded, f32), vm(padded, f32),
            vm((TS, HALF), f32), vm((HALF, TS), f32), vm((2, HALF, TS), f32), vm((2, TS, HALF), f32),
        ]
        + [vm((4, n, TS), f32) for n in widths]
        + [vm((14, 4, n, TS), f32) for n in widths]
        + [vm((4 * n, TS), f32) for n in widths]
        + [
            *[vm((8, HALF), f32)] * 3, *[vm((26, 8, HALF), f32)] * 3,
            *[vm((4, n, TS), f32) for n in later],
            *[vm((14, 4, n, TS), f32) for n in later],
            *[vm((4 * n, TS), f32) for n in later],
            dma((6,)), dma((6,)), dma((6,)), dma((4,)), dma((4,)), dma((3,)), dma((3,)), dma((3,)), dma((3,)),
        ],
        compiler_params=pltpu.CompilerParams(
            collective_id=0, has_side_effects=True, vmem_limit_bytes=48 * 2**20
        ),
    )(neighbours, right_side, pixel_weight, noise_diag, noise_corr)


def solution(mesh):
    placed = (
        P(None, ("tile", "sub"), None),
        P(("tile", "sub"), None),
        P(None, ("tile", "sub"), None),
        P(("tile", "sub"), None),
        P(),
    )
    return jax.shard_map(
        body,
        mesh=mesh,
        in_specs=placed,
        out_specs=(P(None, ("tile", "sub"), None), P(None, ("tile", "sub"), None)),
        check_vma=False,
    )
```

```python
import functools

import jax
import jax.numpy as jnp
from jax import lax
from jax.experimental import pallas as pl
from jax.experimental.pallas import tpu as pltpu
from jax.sharding import PartitionSpec as P

MASS = 0.05
OMEGA = 0.8
KEEP = 1.0 - OMEGA
CENTRE = MASS + 4.0
TS = 256
HALF = 128
TILES = 128
CHUNK = 8
CHUNKS = TS // CHUNK
BATCH = 8
MESH = pl.DeviceIdType.MESH

LINE_OFFS = [-3, -2, -1, 1, 2, 3] + [64 + d for d in range(-3, 4)]
CORNER_OFFS = [-6, -5, -4, -3, -2, -1, 1, 2, 3, 4, 5, 6] + [64 + d for d in range(-6, 7)]


def slot_of(distance, reach):
    d = lax.rem(distance + TILES, TILES)
    far = d - (64 - reach) + 2 * reach
    near = jnp.where(d <= reach, d + reach - 1, d - (TILES - reach))
    slot = jnp.where((d <= reach) | (d >= TILES - reach), near, far)
    slot = jnp.where(d == 0, 4 * reach + 1, slot)
    return jnp.minimum(jnp.maximum(slot, 0), 4 * reach + 1)


def lanes(rows, cols):
    return lax.broadcasted_iota(jnp.int32, (rows, cols), 1)


def pair_sum(x):
    lane = lanes(CHUNK, TS)
    x = x + jnp.where(lane % 2 == 0, pltpu.roll(x, TS - 1, 1), pltpu.roll(x, 1, 1))
    row = lax.broadcasted_iota(jnp.int32, (CHUNK, TS), 0)
    return x + jnp.where(row % 2 == 0, pltpu.roll(x, CHUNK - 1, 0), pltpu.roll(x, 1, 0))


def smoother_terms(stiffness, w, n0, n1, cross, f0, f1):
    diag = (stiffness * CENTRE) * w * w
    b00, b11 = diag + n0, diag + n1
    scale = OMEGA / (b00 * b11 - cross * cross)
    k00, k11, k01 = scale * b11, scale * b00, -(scale * cross)
    v0 = w * (k00 * f0 + k01 * f1)
    v1 = w * (k01 * f0 + k11 * f1)
    ww = stiffness * w * w
    return v0, v1, ww * k00, ww * k11, ww * k01


def kernel(
    nb, rs_in, w_in, nd_in, nc_in, sol_out, mis_out,
    rs, wt, nd, nc, iw, kf, kc, sf, sc, wiw, va, vb, ca, cb,
    ec, ect, hs, hc, st1, st2, st3, st4, re1, re2, re3, re4, nb1, nb2, nb3, nb4,
    cs1, cs2, cs3, cr1, cr2, cr3, lsem, psem, prem, ssem, rsem, cssem, crsem,
):
    cst, cre = (cs1, cs2, cs3), (cr1, cr2, cr3)
    t = lax.axis_index("tile")
    c = lax.axis_index("sub")
    band = pl.multiple_of(c * HALF, HALF)

    def tile_at(offset):
        return (lax.rem(t + (offset + TILES), TILES), c)

    barrier = pltpu.get_barrier_semaphore()
    for o in CORNER_OFFS:
        pl.semaphore_signal(barrier, inc=1, device_id=tile_at(o), device_id_type=MESH)
    pl.semaphore_signal(barrier, inc=1, device_id=(t, 1 - c), device_id_type=MESH)

    rows = pl.ds(band, HALF)
    moves = [
        (rs_in.at[0], rs.at[0, rows]), (rs_in.at[1], rs.at[1, rows]), (w_in, wt.at[rows]),
        (nd_in.at[0], nd.at[0, rows]), (nd_in.at[1], nd.at[1, rows]), (nc_in, nc.at[rows]),
    ]
    local = [pltpu.make_async_copy(s, d, lsem.at[i]) for i, (s, d) in enumerate(moves)]
    for m in local:
        m.start()
    pl.semaphore_wait(barrier, len(CORNER_OFFS) + 1)
    shared = [
        pltpu.make_async_remote_copy(
            s, d, psem.at[i], prem.at[i], device_id=(t, 1 - c), device_id_type=MESH
        )
        for i, (s, d) in enumerate(moves)
    ]
    for m in shared:
        m.start()

    flip, line_slot, ghost = [], [], {}
    for k in range(4):
        n, f = nb[0, k, t], nb[2, k, t]
        flip.append(f)
        line_slot.append(slot_of(n - t, 3))
        base = 2 if k < 2 else 0
        for e in range(2):
            end = jnp.where(f == 1, 1 - e, e)
            q = base + end
            m, g = nb[0, q, n], nb[2, q, n]
            place = (k ^ 1) % 2
            ghost[k, e] = (slot_of(m - t, 6), end, jnp.where(g == 1, 1 - place, place))

    def send(x, stage, land, width):
        for o in LINE_OFFS:
            i = LINE_OFFS.index((-o + 3) % TILES - 3)
            pltpu.make_async_remote_copy(
                stage, land.at[i], ssem.at[x], rsem.at[x], device_id=tile_at(o), device_id_type=MESH
            ).start()
        if x < 3:
            lane = lanes(2, HALF)
            for k in range(4):
                pair = stage[k, 0:2, :]
                cst[x][2 * k : 2 * k + 2, :] = jnp.where(lane < 64, pair[:, :HALF], pair[:, HALF:])
            for o in CORNER_OFFS:
                i = CORNER_OFFS.index((-o + 6) % TILES - 6)
                pltpu.make_async_remote_copy(
                    cst[x], cre[x].at[i], cssem.at[x], crsem.at[x], device_id=tile_at(o), device_id_type=MESH
                ).start()
            cre[x][len(CORNER_OFFS)] = cst[x][...]
        land[len(LINE_OFFS)] = stage[...]

    def receive(x, land, width, near):
        got = land.at[pl.ds(0, len(LINE_OFFS))]
        pltpu.make_async_copy(got, got, rsem.at[x]).wait()
        for k in range(4):
            near[k * width : (k + 1) * width, :] = land[line_slot[k], k ^ 1]
        back = (HALF - 1) - lanes(8, HALF)
        for b in range(0, 4 * width, 8):
            v = near[b : b + 8, :]
            turned = jnp.concatenate(
                [
                    jnp.take_along_axis(v[:, HALF:], back, axis=1),
                    jnp.take_along_axis(v[:, :HALF], back, axis=1),
                ],
                axis=1,
            )
            side = (lax.broadcasted_iota(jnp.int32, (8, TS), 0) + b) // width
            flag = jnp.where(
                side < 2, jnp.where(side == 0, flip[0], flip[1]), jnp.where(side == 2, flip[2], flip[3])
            )
            near[b : b + 8, :] = jnp.where(flag == 1, turned, v)

    def corners(x):
        got = cre[x].at[pl.ds(0, len(CORNER_OFFS))]
        pltpu.make_async_copy(got, got, crsem.at[x]).wait()
        values = {}
        for k in range(4):
            low = 4 if k < 2 else 0
            for e in range(2):
                slot, end, place = ghost[k, e]
                block = cre[x][slot]
                pair = jnp.where(end == 1, block[low : low + 2, :], block[low + 2 : low + 4, :])
                values[k, e] = jnp.where(place == 1, pair[:, HALF - 1 :], pair[:, :1])
        return values

    def advance(near, width, stage, s, ghosts, outer, terms):
        lane = lanes(1, TS)
        out = []
        for k in range(4):
            line = [near[k * width + j : k * width + j + 1, :] for j in range(2)]
            sums = []
            for j in range(2):
                low = jnp.where(lane < s, ghosts[k, 0][j : j + 1, :], pltpu.roll(line[j], s, 1))
                high = jnp.where(lane >= TS - s, ghosts[k, 1][j : j + 1, :], pltpu.roll(line[j], TS - s, 1))
                beyond = near[k * width + outer + j : k * width + outer + j + 1, :]
                sums.append(low + high + beyond + stage[k, j : j + 1, :])
            start0, start1, k00, k11, k01 = terms(k)
            out.append(
                [
                    KEEP * line[0] + start0 + (k00 * sums[0] + k01 * sums[1]),
                    KEEP * line[1] + start1 + (k01 * sums[0] + k11 * sums[1]),
                ]
            )
        return out

    def set_halo(v, s, lines):
        for j in range(2):
            for i in range(s):
                v[j, 7 - i : 8 - i, :] = lines[0][j]
                v[j, 264 + i : 265 + i, :] = lines[1][j]
                hs[j, i : i + 1, :] = lines[2][j]
                hs[j, HALF - 1 - i : HALF - i, :] = lines[3][j]
            hc[j] = jnp.transpose(hs[j])

    def plain_lines(near, width):
        return [[near[k * width + j : k * width + j + 1, :] for j in range(2)] for k in range(4)]

    def beside(v, j, r, s):
        lane = lanes(CHUNK, TS)
        here = v[j, pl.ds(r + 8, CHUNK), :]
        row = lax.broadcasted_iota(jnp.int32, (CHUNK, TS), 0)
        above = pltpu.roll(jnp.where(row >= CHUNK - s, v[j, pl.ds(r, CHUNK), :], here), s, 0)
        below = pltpu.roll(jnp.where(row < s, v[j, pl.ds(r + 16, CHUNK), :], here), CHUNK - s, 0)
        edge = hc[j, pl.ds(r, CHUNK), :]
        edge = jnp.concatenate([edge, edge], axis=1)
        west = jnp.where(lane < s, edge, pltpu.roll(here, s, 1))
        east = jnp.where(lane >= TS - s, edge, pltpu.roll(here, TS - s, 1))
        return here, (above + below) + (west + east)

    def put_edges(r, q, u, extra=()):
        lane = lanes(CHUNK, HALF)
        out = jnp.where(lane < 64, pltpu.roll(u[:, :HALF], 3, 1), pltpu.roll(u[:, HALF:], HALF - 3, 1))
        out = jnp.where(lane < 3, q[:, :HALF], jnp.where(lane >= HALF - 3, q[:, HALF:], out))
        for i, x in enumerate(extra):
            out = jnp.where(lane == 6 + i, pltpu.roll(x[:, :HALF], 6 + i, 1), out)
            out = jnp.where(lane == HALF - 7 - i, pltpu.roll(x[:, HALF:], HALF - 6 - i, 1), out)
        ec[pl.ds(r, CHUNK), :] = out

    def fill_stage(stage, v, s, second, terms):
        ect[...] = jnp.transpose(ec[...])
        for j in range(2):
            stage[0, j : j + 1, :] = v[j, 8:9, :]
            stage[1, j : j + 1, :] = v[j, 263:264, :]
            stage[2, j : j + 1, :] = ect[3 * j : 3 * j + 1, :]
            stage[3, j : j + 1, :] = ect[127 - 3 * j : 128 - 3 * j, :]
            if second is not None:
                b = second + j
                stage[0, b : b + 1, :] = v[j, 8 + s : 9 + s, :]
                stage[1, b : b + 1, :] = v[j, 263 - s : 264 - s, :]
                stage[2, b : b + 1, :] = ect[3 * j + s : 3 * j + s + 1, :]
                stage[3, b : b + 1, :] = ect[127 - 3 * j - s : 128 - 3 * j - s, :]
        if terms is not None:
            for i in range(3):
                stage[0, 2 + i : 3 + i, :] = terms[i, 0:1, :]
                stage[1, 2 + i : 3 + i, :] = terms[i, TS - 1 : TS, :]
                stage[2, 2 + i : 3 + i, :] = ect[6 + i : 7 + i, :]
                stage[3, 2 + i : 3 + i, :] = ect[121 - i : 122 - i, :]
            stage[:, 7:8, :] = jnp.zeros((4, 1, TS), jnp.float32)

    def over_chunks(step, first=0, count=CHUNKS):
        def body(i, carry):
            for b in range(BATCH):
                step(pl.multiple_of(first + (i * BATCH + b) * CHUNK, CHUNK))
            return carry
        lax.fori_loop(0, count // BATCH, body, 0)

    def sweep(src, start, terms, s, r):
        q, nq = beside(src, 0, r, s)
        u, nu = beside(src, 1, r, s)
        here = pl.ds(r, CHUNK)
        k00, k11, k01 = terms[0, here, :], terms[1, here, :], terms[2, here, :]
        q = KEEP * q + start[0, here, :] + (k00 * nq + k01 * nu)
        u = KEEP * u + start[1, here, :] + (k01 * nq + k11 * nu)
        return q, u

    def residual(src, r):
        here = pl.ds(r, CHUNK)
        q, nq = beside(src, 0, r, 1)
        u, nu = beside(src, 1, r, 1)
        w, cross, inv = wt[here, :], nc[here, :], iw[here, :]
        q0, u0 = q * inv, u * inv
        mq = rs[0, here, :] - (w * (CENTRE * q - nq) + nd[0, here, :] * q0 + cross * u0)
        mu = rs[1, here, :] - (w * (CENTRE * u - nu) + cross * q0 + nd[1, here, :] * u0)
        return mq, mu, q0, u0

    hs[...] = jnp.zeros_like(hs)
    for m in local:
        m.wait()

    def start_fine(r):
        here = pl.ds(r, CHUNK)
        n0, n1, w = nd[0, here, :], nd[1, here, :], wt[here, :]
        cross = nc[here, :] * jnp.sqrt(n0 * n1)
        nc[here, :] = cross
        iw[here, :] = 1.0 / w
        q, u, k00, k11, k01 = smoother_terms(1.0, w, n0, n1, cross, rs[0, here, :], rs[1, here, :])
        kf[0, here, :], kf[1, here, :], kf[2, here, :] = k00, k11, k01
        sf[0, here, :], sf[1, here, :] = q, u
        va[0, pl.ds(r + 8, CHUNK), :], va[1, pl.ds(r + 8, CHUNK), :] = q, u
        put_edges(r, q, u, (k00, k11, k01))

    over_chunks(start_fine, band, CHUNKS // 2)
    for m in shared:
        m.wait()
    over_chunks(start_fine, pl.multiple_of(HALF - band, HALF), CHUNKS // 2)
    fill_stage(st1, va, 1, 5, kf)
    send(0, st1, re1, 8)
    receive(0, re1, 8, nb1)
    set_halo(va, 1, plain_lines(nb1, 8))

    def first_sweep(r):
        q, u = sweep(va, sf, kf, 1, r)
        vb[0, pl.ds(r + 8, CHUNK), :], vb[1, pl.ds(r + 8, CHUNK), :] = q, u

    over_chunks(first_sweep)

    def terms_of(near):
        def terms(k):
            return [near[k * 8 + j : k * 8 + j + 1, :] for j in (0, 1, 2, 3, 4)]
        return terms

    set_halo(vb, 1, advance(nb1, 8, st1, 1, corners(0), 5, terms_of(nb1)))

    def start_coarse(r):
        here = pl.ds(r, CHUNK)
        mq, mu, _, _ = residual(vb, r)
        w = wt[here, :]
        cw = 0.25 * pair_sum(w)
        wiw[here, :] = w / cw
        q, u, k00, k11, k01 = smoother_terms(
            2.0, cw, pair_sum(nd[0, here, :]), pair_sum(nd[1, here, :]), pair_sum(nc[here, :]),
            pair_sum(mq), pair_sum(mu),
        )
        kc[0, here, :], kc[1, here, :], kc[2, here, :] = k00, k11, k01
        sc[0, here, :], sc[1, here, :] = q, u
        ca[0, pl.ds(r + 8, CHUNK), :], ca[1, pl.ds(r + 8, CHUNK), :] = q, u
        put_edges(r, q, u, (k00, k11, k01))

    over_chunks(start_coarse)
    fill_stage(st2, ca, 2, 5, kc)
    send(1, st2, re2, 8)
    receive(1, re2, 8, nb2)
    set_halo(ca, 2, plain_lines(nb2, 8))

    def coarse_sweep(r):
        q, u = sweep(ca, sc, kc, 2, r)
        cb[0, pl.ds(r + 8, CHUNK), :], cb[1, pl.ds(r + 8, CHUNK), :] = q, u

    over_chunks(coarse_sweep)
    set_halo(cb, 2, advance(nb2, 8, st2, 2, corners(1), 5, terms_of(nb2)))

    def correct(r):
        q, u = sweep(cb, sc, kc, 2, r)
        up = wiw[pl.ds(r, CHUNK), :]
        here = pl.ds(r + 8, CHUNK)
        q, u = vb[0, here, :] + up * q, vb[1, here, :] + up * u
        va[0, here, :], va[1, here, :] = q, u
        put_edges(r, q, u)

    over_chunks(correct)
    fill_stage(st3, va, 1, 2, None)
    send(2, st3, re3, 4)
    receive(2, re3, 4, nb3)
    set_halo(va, 1, plain_lines(nb3, 4))
    over_chunks(first_sweep)
    set_halo(vb, 1, advance(nb3, 4, st3, 1, corners(2), 2, terms_of(nb1)))

    def last_sweep(r):
        q, u = sweep(vb, sf, kf, 1, r)
        va[0, pl.ds(r + 8, CHUNK), :], va[1, pl.ds(r + 8, CHUNK), :] = q, u
        put_edges(r, q, u)

    over_chunks(last_sweep)
    fill_stage(st4, va, 1, None, None)
    send(3, st4, re4, 2)
    receive(3, re4, 2, nb4)
    set_halo(va, 1, plain_lines(nb4, 2))

    def finish(i):
        r = pl.multiple_of(band + i, CHUNK)
        mq, mu, q, u = residual(va, r)
        here = pl.ds(i, CHUNK)
        sol_out[0, here, :], sol_out[1, here, :] = q, u
        mis_out[0, here, :], mis_out[1, here, :] = mq, mu

    over_chunks(finish, 0, HALF // CHUNK)

    for x, land in enumerate((re1, re2, re3, re4)):
        sent = land.at[pl.ds(0, len(LINE_OFFS))]
        pltpu.make_async_copy(sent, sent, ssem.at[x]).wait()
        if x < 3:
            sent = cre[x].at[pl.ds(0, len(CORNER_OFFS))]
            pltpu.make_async_copy(sent, sent, cssem.at[x]).wait()


def body(right_side, pixel_weight, noise_diag, noise_corr, neighbours):
    f32 = jnp.float32
    vm = pltpu.VMEM
    plane, pair, triple, padded = (TS, TS), (2, TS, TS), (3, TS, TS), (2, TS + 16, TS)
    hbm = pl.BlockSpec(memory_space=pl.ANY)
    widths = (8, 8, 4, 2)
    dma = pltpu.SemaphoreType.DMA
    return pl.pallas_call(
        kernel,
        out_shape=[jax.ShapeDtypeStruct((2, HALF, TS), f32)] * 2,
        in_specs=[pl.BlockSpec(memory_space=pltpu.SMEM), hbm, hbm, hbm, hbm],
        out_specs=[pl.BlockSpec(memory_space=pltpu.VMEM)] * 2,
        scratch_shapes=[
            vm(pair, f32), vm(plane, f32), vm(pair, f32), vm(plane, f32), vm(plane, f32),
            vm(triple, f32), vm(triple, f32), vm(pair, f32), vm(pair, f32), vm(plane, f32),
            vm(padded, f32), vm(padded, f32), vm(padded, f32), vm(padded, f32),
            vm((TS, HALF), f32), vm((HALF, TS), f32), vm((2, HALF, TS), f32), vm((2, TS, HALF), f32),
        ]
        + [vm((4, n, TS), f32) for n in widths]
        + [vm((14, 4, n, TS), f32) for n in widths]
        + [vm((4 * n, TS), f32) for n in widths]
        + [
            *[vm((8, HALF), f32)] * 3, *[vm((26, 8, HALF), f32)] * 3,
            dma((6,)), dma((6,)), dma((6,)), dma((4,)), dma((4,)), dma((3,)), dma((3,)),
        ],
        compiler_params=pltpu.CompilerParams(
            collective_id=0, has_side_effects=True, vmem_limit_bytes=48 * 2**20
        ),
    )(neighbours, right_side, pixel_weight, noise_diag, noise_corr)


def solution(mesh):
    placed = (
        P(None, ("tile", "sub"), None),
        P(("tile", "sub"), None),
        P(None, ("tile", "sub"), None),
        P(("tile", "sub"), None),
        P(),
    )
    return jax.shard_map(
        body,
        mesh=mesh,
        in_specs=placed,
        out_specs=(P(None, ("tile", "sub"), None), P(None, ("tile", "sub"), None)),
        check_vma=False,
    )
```

```python
import functools

import jax
import jax.numpy as jnp
from jax import lax
from jax.experimental import pallas as pl
from jax.experimental.pallas import tpu as pltpu
from jax.sharding import PartitionSpec as P

MASS = 0.05
OMEGA = 0.8
KEEP = 1.0 - OMEGA
CENTRE = MASS + 4.0
TS = 256
HALF = 128
TILES = 128
CHUNK = 8
CHUNKS = TS // CHUNK
BATCH = 8
MESH = pl.DeviceIdType.MESH

LINE_OFFS = [-3, -2, -1, 1, 2, 3] + [64 + d for d in range(-3, 4)]
CORNER_OFFS = [-6, -5, -4, -3, -2, -1, 1, 2, 3, 4, 5, 6] + [64 + d for d in range(-6, 7)]


def slot_of(distance, reach):
    d = lax.rem(distance + TILES, TILES)
    far = d - (64 - reach) + 2 * reach
    near = jnp.where(d <= reach, d + reach - 1, d - (TILES - reach))
    slot = jnp.where((d <= reach) | (d >= TILES - reach), near, far)
    slot = jnp.where(d == 0, 4 * reach + 1, slot)
    return jnp.minimum(jnp.maximum(slot, 0), 4 * reach + 1)


def lanes(rows, cols):
    return lax.broadcasted_iota(jnp.int32, (rows, cols), 1)


def pair_sum(x):
    lane = lanes(CHUNK, TS)
    x = x + jnp.where(lane % 2 == 0, pltpu.roll(x, TS - 1, 1), pltpu.roll(x, 1, 1))
    row = lax.broadcasted_iota(jnp.int32, (CHUNK, TS), 0)
    return x + jnp.where(row % 2 == 0, pltpu.roll(x, CHUNK - 1, 0), pltpu.roll(x, 1, 0))


def smoother_terms(stiffness, w, n0, n1, cross):
    ww = stiffness * w * w
    diag = CENTRE * ww
    b00, b11 = diag + n0, diag + n1
    scale = ww * (OMEGA / (b00 * b11 - cross * cross))
    return scale * b11, scale * b00, -(scale * cross)


def kernel(
    nb, rs_in, w_in, nd_in, nc_in, sol_out, mis_out,
    rs, wt, nd, nc, iw, kf, kc, sf, sc, wiw, icw, va, vb, ca, cb,
    ec, ect, hs, hc, st1, st2, st3, st4, re1, re2, re3, re4, nb1, nb2, nb3, nb4,
    cs1, cs2, cs3, cr1, cr2, cr3, lsem, psem, prem, ssem, rsem, cssem, crsem,
):
    cst, cre = (cs1, cs2, cs3), (cr1, cr2, cr3)
    t = lax.axis_index("tile")
    c = lax.axis_index("sub")
    band = pl.multiple_of(c * HALF, HALF)

    def tile_at(offset):
        return (lax.rem(t + (offset + TILES), TILES), c)

    barrier = pltpu.get_barrier_semaphore()
    for o in CORNER_OFFS:
        pl.semaphore_signal(barrier, inc=1, device_id=tile_at(o), device_id_type=MESH)
    pl.semaphore_signal(barrier, inc=1, device_id=(t, 1 - c), device_id_type=MESH)

    rows = pl.ds(band, HALF)
    moves = [
        (rs_in.at[0], rs.at[0, rows]), (rs_in.at[1], rs.at[1, rows]), (w_in, wt.at[rows]),
        (nd_in.at[0], nd.at[0, rows]), (nd_in.at[1], nd.at[1, rows]), (nc_in, nc.at[rows]),
    ]
    local = [pltpu.make_async_copy(s, d, lsem.at[i]) for i, (s, d) in enumerate(moves)]
    for m in local:
        m.start()
    pl.semaphore_wait(barrier, len(CORNER_OFFS) + 1)
    shared = [
        pltpu.make_async_remote_copy(
            s, d, psem.at[i], prem.at[i], device_id=(t, 1 - c), device_id_type=MESH
        )
        for i, (s, d) in enumerate(moves)
    ]
    for m in shared:
        m.start()

    flip, line_slot, ghost = [], [], {}
    for k in range(4):
        n, f = nb[0, k, t], nb[2, k, t]
        flip.append(f)
        line_slot.append(slot_of(n - t, 3))
        base = 2 if k < 2 else 0
        for e in range(2):
            end = jnp.where(f == 1, 1 - e, e)
            q = base + end
            m, g = nb[0, q, n], nb[2, q, n]
            place = (k ^ 1) % 2
            ghost[k, e] = (slot_of(m - t, 6), end, jnp.where(g == 1, 1 - place, place))

    def send(x, stage, land, width):
        for o in LINE_OFFS:
            i = LINE_OFFS.index((-o + 3) % TILES - 3)
            pltpu.make_async_remote_copy(
                stage, land.at[i], ssem.at[x], rsem.at[x], device_id=tile_at(o), device_id_type=MESH
            ).start()
        if x < 3:
            lane = lanes(2, HALF)
            for k in range(4):
                pair = stage[k, 0:2, :]
                cst[x][2 * k : 2 * k + 2, :] = jnp.where(lane < 64, pair[:, :HALF], pair[:, HALF:])
            for o in CORNER_OFFS:
                i = CORNER_OFFS.index((-o + 6) % TILES - 6)
                pltpu.make_async_remote_copy(
                    cst[x], cre[x].at[i], cssem.at[x], crsem.at[x], device_id=tile_at(o), device_id_type=MESH
                ).start()
            cre[x][len(CORNER_OFFS)] = cst[x][...]
        land[len(LINE_OFFS)] = stage[...]

    def receive(x, land, width, near):
        got = land.at[pl.ds(0, len(LINE_OFFS))]
        pltpu.make_async_copy(got, got, rsem.at[x]).wait()
        for k in range(4):
            near[k * width : (k + 1) * width, :] = land[line_slot[k], k ^ 1]
        back = (HALF - 1) - lanes(8, HALF)
        for b in range(0, 4 * width, 8):
            v = near[b : b + 8, :]
            turned = jnp.concatenate(
                [
                    jnp.take_along_axis(v[:, HALF:], back, axis=1),
                    jnp.take_along_axis(v[:, :HALF], back, axis=1),
                ],
                axis=1,
            )
            side = (lax.broadcasted_iota(jnp.int32, (8, TS), 0) + b) // width
            flag = jnp.where(
                side < 2, jnp.where(side == 0, flip[0], flip[1]), jnp.where(side == 2, flip[2], flip[3])
            )
            near[b : b + 8, :] = jnp.where(flag == 1, turned, v)

    def corners(x):
        got = cre[x].at[pl.ds(0, len(CORNER_OFFS))]
        pltpu.make_async_copy(got, got, crsem.at[x]).wait()
        values = {}
        for k in range(4):
            low = 4 if k < 2 else 0
            for e in range(2):
                slot, end, place = ghost[k, e]
                block = cre[x][slot]
                pair = jnp.where(end == 1, block[low : low + 2, :], block[low + 2 : low + 4, :])
                values[k, e] = jnp.where(place == 1, pair[:, HALF - 1 :], pair[:, :1])
        return values

    def advance(near, width, stage, s, ghosts, outer, terms):
        lane = lanes(1, TS)
        out = []
        for k in range(4):
            line = [near[k * width + j : k * width + j + 1, :] for j in range(2)]
            sums = []
            for j in range(2):
                low = jnp.where(lane < s, ghosts[k, 0][j : j + 1, :], pltpu.roll(line[j], s, 1))
                high = jnp.where(lane >= TS - s, ghosts[k, 1][j : j + 1, :], pltpu.roll(line[j], TS - s, 1))
                beyond = near[k * width + outer + j : k * width + outer + j + 1, :]
                sums.append(low + high + beyond + stage[k, j : j + 1, :])
            start0, start1, k00, k11, k01 = terms(k)
            out.append(
                [
                    KEEP * line[0] + start0 + (k00 * sums[0] + k01 * sums[1]),
                    KEEP * line[1] + start1 + (k01 * sums[0] + k11 * sums[1]),
                ]
            )
        return out

    def set_halo(v, s, lines):
        for j in range(2):
            for i in range(s):
                v[j, 7 - i : 8 - i, :] = lines[0][j]
                v[j, 264 + i : 265 + i, :] = lines[1][j]
                hs[j, i : i + 1, :] = lines[2][j]
                hs[j, HALF - 1 - i : HALF - i, :] = lines[3][j]
            hc[j] = jnp.transpose(hs[j])

    def plain_lines(near, width):
        return [[near[k * width + j : k * width + j + 1, :] for j in range(2)] for k in range(4)]

    def beside(v, j, r, s):
        lane = lanes(CHUNK, TS)
        here = v[j, pl.ds(r + 8, CHUNK), :]
        row = lax.broadcasted_iota(jnp.int32, (CHUNK, TS), 0)
        above = pltpu.roll(jnp.where(row >= CHUNK - s, v[j, pl.ds(r, CHUNK), :], here), s, 0)
        below = pltpu.roll(jnp.where(row < s, v[j, pl.ds(r + 16, CHUNK), :], here), CHUNK - s, 0)
        edge = hc[j, pl.ds(r, CHUNK), :]
        edge = jnp.concatenate([edge, edge], axis=1)
        west = jnp.where(lane < s, edge, pltpu.roll(here, s, 1))
        east = jnp.where(lane >= TS - s, edge, pltpu.roll(here, TS - s, 1))
        return here, (above + below) + (west + east)

    def put_edges(r, q, u, extra=()):
        lane = lanes(CHUNK, HALF)
        out = jnp.where(lane < 64, pltpu.roll(u[:, :HALF], 3, 1), pltpu.roll(u[:, HALF:], HALF - 3, 1))
        out = jnp.where(lane < 3, q[:, :HALF], jnp.where(lane >= HALF - 3, q[:, HALF:], out))
        for i, x in enumerate(extra):
            out = jnp.where(lane == 6 + i, pltpu.roll(x[:, :HALF], 6 + i, 1), out)
            out = jnp.where(lane == HALF - 7 - i, pltpu.roll(x[:, HALF:], HALF - 6 - i, 1), out)
        ec[pl.ds(r, CHUNK), :] = out

    def fill_stage(stage, v, s, second, terms):
        ect[...] = jnp.transpose(ec[...])
        for j in range(2):
            stage[0, j : j + 1, :] = v[j, 8:9, :]
            stage[1, j : j + 1, :] = v[j, 263:264, :]
            stage[2, j : j + 1, :] = ect[3 * j : 3 * j + 1, :]
            stage[3, j : j + 1, :] = ect[127 - 3 * j : 128 - 3 * j, :]
            if second is not None:
                b = second + j
                stage[0, b : b + 1, :] = v[j, 8 + s : 9 + s, :]
                stage[1, b : b + 1, :] = v[j, 263 - s : 264 - s, :]
                stage[2, b : b + 1, :] = ect[3 * j + s : 3 * j + s + 1, :]
                stage[3, b : b + 1, :] = ect[127 - 3 * j - s : 128 - 3 * j - s, :]
        if terms is not None:
            for i in range(3):
                stage[0, 2 + i : 3 + i, :] = terms[i, 0:1, :]
                stage[1, 2 + i : 3 + i, :] = terms[i, TS - 1 : TS, :]
                stage[2, 2 + i : 3 + i, :] = ect[6 + i : 7 + i, :]
                stage[3, 2 + i : 3 + i, :] = ect[121 - i : 122 - i, :]
            stage[:, 7:8, :] = jnp.zeros((4, 1, TS), jnp.float32)

    def over_chunks(step, first=0, count=CHUNKS):
        def body(i, carry):
            for b in range(BATCH):
                step(pl.multiple_of(first + (i * BATCH + b) * CHUNK, CHUNK))
            return carry
        lax.fori_loop(0, count // BATCH, body, 0)

    def sweep(src, start, terms, s, r):
        q, nq = beside(src, 0, r, s)
        u, nu = beside(src, 1, r, s)
        here = pl.ds(r, CHUNK)
        k00, k11, k01 = terms[0, here, :], terms[1, here, :], terms[2, here, :]
        q = KEEP * q + start[0, here, :] + (k00 * nq + k01 * nu)
        u = KEEP * u + start[1, here, :] + (k01 * nq + k11 * nu)
        return q, u

    def residual(src, r):
        here = pl.ds(r, CHUNK)
        q, nq = beside(src, 0, r, 1)
        u, nu = beside(src, 1, r, 1)
        w, cross, inv = wt[here, :], nc[here, :], iw[here, :]
        q0, u0 = q * inv, u * inv
        mq = rs[0, here, :] - (w * (CENTRE * q - nq) + nd[0, here, :] * q0 + cross * u0)
        mu = rs[1, here, :] - (w * (CENTRE * u - nu) + cross * q0 + nd[1, here, :] * u0)
        return mq, mu, q0, u0

    hs[...] = jnp.zeros_like(hs)
    for m in local:
        m.wait()

    def start_fine(r):
        here = pl.ds(r, CHUNK)
        n0, n1, w = nd[0, here, :], nd[1, here, :], wt[here, :]
        cross = nc[here, :] * jnp.sqrt(n0 * n1)
        nc[here, :] = cross
        inv = 1.0 / w
        iw[here, :] = inv
        k00, k11, k01 = smoother_terms(1.0, w, n0, n1, cross)
        f0, f1 = rs[0, here, :] * inv, rs[1, here, :] * inv
        q, u = k00 * f0 + k01 * f1, k01 * f0 + k11 * f1
        kf[0, here, :], kf[1, here, :], kf[2, here, :] = k00, k11, k01
        sf[0, here, :], sf[1, here, :] = q, u
        va[0, pl.ds(r + 8, CHUNK), :], va[1, pl.ds(r + 8, CHUNK), :] = q, u
        put_edges(r, q, u, (k00, k11, k01))

    over_chunks(start_fine, band, CHUNKS // 2)
    for m in shared:
        m.wait()
    over_chunks(start_fine, pl.multiple_of(HALF - band, HALF), CHUNKS // 2)
    fill_stage(st1, va, 1, 5, kf)
    send(0, st1, re1, 8)

    def coarse_terms(r):
        here = pl.ds(r, CHUNK)
        w = wt[here, :]
        cw = 0.25 * pair_sum(w)
        icw[here, :] = 0.5 / cw
        wiw[here, :] = w / cw
        kc[0, here, :], kc[1, here, :], kc[2, here, :] = smoother_terms(
            2.0, cw, pair_sum(nd[0, here, :]), pair_sum(nd[1, here, :]), pair_sum(nc[here, :])
        )

    over_chunks(coarse_terms)
    receive(0, re1, 8, nb1)
    set_halo(va, 1, plain_lines(nb1, 8))

    def first_sweep(r):
        q, u = sweep(va, sf, kf, 1, r)
        vb[0, pl.ds(r + 8, CHUNK), :], vb[1, pl.ds(r + 8, CHUNK), :] = q, u

    over_chunks(first_sweep)

    def terms_of(near):
        def terms(k):
            return [near[k * 8 + j : k * 8 + j + 1, :] for j in (0, 1, 2, 3, 4)]
        return terms

    set_halo(vb, 1, advance(nb1, 8, st1, 1, corners(0), 5, terms_of(nb1)))

    def start_coarse(r):
        here = pl.ds(r, CHUNK)
        mq, mu, _, _ = residual(vb, r)
        inv = icw[here, :]
        f0, f1 = pair_sum(mq) * inv, pair_sum(mu) * inv
        k00, k11, k01 = kc[0, here, :], kc[1, here, :], kc[2, here, :]
        q, u = k00 * f0 + k01 * f1, k01 * f0 + k11 * f1
        sc[0, here, :], sc[1, here, :] = q, u
        ca[0, pl.ds(r + 8, CHUNK), :], ca[1, pl.ds(r + 8, CHUNK), :] = q, u
        put_edges(r, q, u, (k00, k11, k01))

    over_chunks(start_coarse)
    fill_stage(st2, ca, 2, 5, kc)
    send(1, st2, re2, 8)
    receive(1, re2, 8, nb2)
    set_halo(ca, 2, plain_lines(nb2, 8))

    def coarse_sweep(r):
        q, u = sweep(ca, sc, kc, 2, r)
        cb[0, pl.ds(r + 8, CHUNK), :], cb[1, pl.ds(r + 8, CHUNK), :] = q, u

    over_chunks(coarse_sweep)
    set_halo(cb, 2, advance(nb2, 8, st2, 2, corners(1), 5, terms_of(nb2)))

    def correct(r):
        q, u = sweep(cb, sc, kc, 2, r)
        up = wiw[pl.ds(r, CHUNK), :]
        here = pl.ds(r + 8, CHUNK)
        q, u = vb[0, here, :] + up * q, vb[1, here, :] + up * u
        va[0, here, :], va[1, here, :] = q, u
        put_edges(r, q, u)

    over_chunks(correct)
    fill_stage(st3, va, 1, 2, None)
    send(2, st3, re3, 4)
    receive(2, re3, 4, nb3)
    set_halo(va, 1, plain_lines(nb3, 4))
    over_chunks(first_sweep)
    set_halo(vb, 1, advance(nb3, 4, st3, 1, corners(2), 2, terms_of(nb1)))

    def last_sweep(r):
        q, u = sweep(vb, sf, kf, 1, r)
        va[0, pl.ds(r + 8, CHUNK), :], va[1, pl.ds(r + 8, CHUNK), :] = q, u
        put_edges(r, q, u)

    over_chunks(last_sweep)
    fill_stage(st4, va, 1, None, None)
    send(3, st4, re4, 2)
    receive(3, re4, 2, nb4)
    set_halo(va, 1, plain_lines(nb4, 2))

    def finish(i):
        r = pl.multiple_of(band + i, CHUNK)
        mq, mu, q, u = residual(va, r)
        here = pl.ds(i, CHUNK)
        sol_out[0, here, :], sol_out[1, here, :] = q, u
        mis_out[0, here, :], mis_out[1, here, :] = mq, mu

    over_chunks(finish, 0, HALF // CHUNK)

    for x, land in enumerate((re1, re2, re3, re4)):
        sent = land.at[pl.ds(0, len(LINE_OFFS))]
        pltpu.make_async_copy(sent, sent, ssem.at[x]).wait()
        if x < 3:
            sent = cre[x].at[pl.ds(0, len(CORNER_OFFS))]
            pltpu.make_async_copy(sent, sent, cssem.at[x]).wait()


def body(right_side, pixel_weight, noise_diag, noise_corr, neighbours):
    f32 = jnp.float32
    vm = pltpu.VMEM
    plane, pair, triple, padded = (TS, TS), (2, TS, TS), (3, TS, TS), (2, TS + 16, TS)
    hbm = pl.BlockSpec(memory_space=pl.ANY)
    widths = (8, 8, 4, 2)
    dma = pltpu.SemaphoreType.DMA
    return pl.pallas_call(
        kernel,
        out_shape=[jax.ShapeDtypeStruct((2, HALF, TS), f32)] * 2,
        in_specs=[pl.BlockSpec(memory_space=pltpu.SMEM), hbm, hbm, hbm, hbm],
        out_specs=[pl.BlockSpec(memory_space=pltpu.VMEM)] * 2,
        scratch_shapes=[
            vm(pair, f32), vm(plane, f32), vm(pair, f32), vm(plane, f32), vm(plane, f32),
            vm(triple, f32), vm(triple, f32), vm(pair, f32), vm(pair, f32), vm(plane, f32), vm(plane, f32),
            vm(padded, f32), vm(padded, f32), vm(padded, f32), vm(padded, f32),
            vm((TS, HALF), f32), vm((HALF, TS), f32), vm((2, HALF, TS), f32), vm((2, TS, HALF), f32),
        ]
        + [vm((4, n, TS), f32) for n in widths]
        + [vm((14, 4, n, TS), f32) for n in widths]
        + [vm((4 * n, TS), f32) for n in widths]
        + [
            *[vm((8, HALF), f32)] * 3, *[vm((26, 8, HALF), f32)] * 3,
            dma((6,)), dma((6,)), dma((6,)), dma((4,)), dma((4,)), dma((3,)), dma((3,)),
        ],
        compiler_params=pltpu.CompilerParams(
            collective_id=0, has_side_effects=True, vmem_limit_bytes=48 * 2**20
        ),
    )(neighbours, right_side, pixel_weight, noise_diag, noise_corr)


def solution(mesh):
    placed = (
        P(None, ("tile", "sub"), None),
        P(("tile", "sub"), None),
        P(None, ("tile", "sub"), None),
        P(("tile", "sub"), None),
        P(),
    )
    return jax.shard_map(
        body,
        mesh=mesh,
        in_specs=placed,
        out_specs=(P(None, ("tile", "sub"), None), P(None, ("tile", "sub"), None)),
        check_vma=False,
    )
```
